32 devices in a mesh: mem: 8 (over z, y), lat: 4 (over x, core).
Axes of the slice: x: 2, y: 2, z: 4, core: 2. Of those that a mesh axis runs over, the one named last changes fastest.
Arguments:
- prior_sample_states: bfloat16 [16, 2, 16, 1024], P('mem', None, 'lat'), may hold values from -6 to 6
- wind_cfl_ratios: float32 [2, 16, 1024], P(None, 'lat'), may hold values from -0.45 to 0.45
- obs_cell: int32 [4, 2048], P('lat', 'mem'), may hold values from 0 to 511
- obs_value: float32 [4, 2048], P('lat', 'mem'), may hold values from -6 to 6
- obs_precision: float32 [4, 2048], P('lat', 'mem'), may hold values from 0.25 to 4
- neighbours: int32 [16, 8, 512], P('lat', 'mem'), may hold values from 0 to 1279, as said below
- obs_counts: int32 [16, 8], P('lat', 'mem'), may hold values from 128 to 512, as said below
Outputs:
- analysis: bfloat16 [16, 2, 16, 1024], P('mem', None, 'lat')
The draws below stay inside these ranges and needn't reach their ends.
Inputs may be any that keep to these rules, and one draw needn't show every extreme that they name: `obs_counts`: in every tile some block's list has all 512 slots live. `neighbours`: the 512 entries of one list are distinct and index the extended set of its tile.
All inputs are finite; a program needn't handle non-finite values. Where the reference program divides by a largest or mean magnitude, that divisor is 1e-20 or more.
Results may differ from the reference program's by a relative error of at most 0.0053.
Values may be sent and summed in bfloat16 or wider, within the bound.
A program may use at most 64 MiB of HBM per device.

```python
import math
import jax
import jax.numpy as jnp
from jax import lax

ENS = 16
ZONE_HEIGHT = 4
PATCH_WIDTH = 128
OBS_DEV = 256
KNB = 512
SECTIONS = 4
NS_ITERS = 6
MESH_HEIGHT = 16
MESH_WIDTH = 1024
LOC_ROWS = 2
LOC_COLS = 64
N_MEM = 8
N_LAT = 4


def draw_neighbours(key, part):
    extent = 5 * OBS_DEV
    tile_total = MESH_WIDTH // PATCH_WIDTH
    scores = jax.random.randint(key, (MESH_HEIGHT, tile_total, extent), 0, 1024)
    scores = scores * extent + jnp.arange(extent, dtype=jnp.int32)
    top_values, top_index = lax.top_k(scores, KNB)
    return top_index.astype(jnp.int32)


def draw_obs_counts(key, part):
    band_total = MESH_HEIGHT // ZONE_HEIGHT
    tile_total = MESH_WIDTH // PATCH_WIDTH
    counts = jax.random.randint(key, (band_total, ZONE_HEIGHT, tile_total), KNB // 4, KNB + 1)
    picked = jax.random.randint(jax.random.fold_in(key, 7), (band_total, 1, tile_total), 0, ZONE_HEIGHT)
    counts = jnp.where(jnp.arange(ZONE_HEIGHT, dtype=jnp.int32)[None, :, None] == picked, KNB, counts)
    return counts.reshape(MESH_HEIGHT, tile_total).astype(jnp.int32)


def plant(values, key, low, top_value):
    place = [jax.random.randint(jax.random.fold_in(key, axis), (), 0, length) for axis, length in enumerate(values.shape)]
    widest = values.shape.index(max(values.shape))
    beside = place[:widest] + [(place[widest] + 1) % values.shape[widest]] + place[widest + 1:]
    return values.at[tuple(place)].set(low).at[tuple(beside)].set(top_value)


def levels(rng, shape, split, least, high):
    gain, own = 1.0, jax.random.fold_in(rng, 6)
    for position, blocks in split:
        heights = jnp.exp(jax.random.uniform(jax.random.fold_in(own, position), (blocks,), jnp.float32, least / len(split), high / len(split)))
        gain = gain * jnp.repeat(heights, shape[position] // blocks).reshape([-1 if axis == position else 1 for axis in range(len(shape))])
    return gain


def scatter_about(own_key, dims, width, reach, cuts=(), kind=jnp.bfloat16):
    result = jax.random.normal(own_key, dims, jnp.float32) * width
    if len(cuts) > 0:
        result = levels(own_key, dims, cuts, -0.22, 0.18) * result
    return jnp.clip(result, min=-reach, max=reach).astype(kind)


def setup_inputs(seed: int = 0) -> dict:
    arg_keys = jax.random.split(jax.random.key(seed), 8)
    return {
        "prior_sample_states": scatter_about(arg_keys[0], (ENS, 2, MESH_HEIGHT, MESH_WIDTH), 1.0, 6.0, ((0, 8), (2, 4))),
        "wind_cfl_ratios": jnp.clip(jax.random.uniform(arg_keys[1], (2, MESH_HEIGHT, MESH_WIDTH), jnp.float32, -0.45, 0.45) * levels(arg_keys[1], (2, MESH_HEIGHT, MESH_WIDTH), ((1, 4),), -0.4, 0.0), -0.45, 0.45),
        "obs_cell": plant(jax.random.randint(arg_keys[2], (N_LAT, N_MEM * OBS_DEV), 0, ZONE_HEIGHT * PATCH_WIDTH), jax.random.fold_in(arg_keys[2], 1), 0, (ZONE_HEIGHT * PATCH_WIDTH) - 1).astype(jnp.int32),
        "obs_value": scatter_about(arg_keys[3], (N_LAT, N_MEM * OBS_DEV), 1.0, 6.0, ((0, 4), (1, 8)), jnp.float32),
        "obs_precision": jnp.clip(jnp.exp(math.log(4.0) - 2.7725887 * jax.random.uniform(arg_keys[4], (N_LAT, N_MEM * OBS_DEV), jnp.float32) ** levels(arg_keys[4], (N_LAT, N_MEM * OBS_DEV), ((0, 4), (1, 8)), -0.2, 0.2)), 0.25, 4.0),
        "neighbours": draw_neighbours(jax.random.fold_in(arg_keys[7], 71), 0),
        "obs_counts": draw_obs_counts(jax.random.fold_in(arg_keys[7], 71), 0),
    }


KAPPA = (0.025, 0.0125)
HIGHEST = lax.Precision.HIGHEST

def index_tuple(*entries):
    return tuple((jnp.asarray(entry).astype(jnp.int32) for entry in entries))

def advance(padded, east_wind, north_wind, diffusion):
    centre = padded[:, 1:-1, :]
    north_row = padded[:, 2:, :]
    south_row = padded[:, :-2, :]
    widened = jnp.pad(centre, ((0, 0), (0, 0), (1, 1)))
    west_cell = widened[:, :, :-2]
    east_cell = widened[:, :, 2:]
    transport = jnp.maximum(east_wind, 0.0) * (centre - west_cell) + jnp.minimum(east_wind, 0.0) * (east_cell - centre) + jnp.maximum(north_wind, 0.0) * (centre - south_row) + jnp.minimum(north_wind, 0.0) * (north_row - centre)
    return centre - transport + diffusion * (north_row + south_row + east_cell + west_cell - 4.0 * centre)

def place_piece(piece, sample_realizations, row_shift, col_shift):
    return jnp.concatenate([piece[:sample_realizations + 2], piece[sample_realizations + 2:sample_realizations + 3] + row_shift, piece[sample_realizations + 3:] + col_shift], axis=0)

def analyze(mesh_patch, extended, block_lists, block_counts):
    sample_realizations = mesh_patch.shape[0]
    analysis_block_count = mesh_patch.shape[2]
    tile_width = mesh_patch.shape[3]
    obs_ens = extended[:sample_realizations]
    obs_mean = lax.optimization_barrier(jnp.mean(obs_ens, axis=0))
    spread = obs_ens - obs_mean
    innovation = extended[sample_realizations] - obs_mean
    precision = extended[sample_realizations + 1]
    obs_row = extended[sample_realizations + 2]
    obs_col = extended[sample_realizations + 3]
    chosen = jnp.take(spread, block_lists, axis=1)
    active = (jnp.arange(block_lists.shape[1], dtype=jnp.int32)[None, :] < block_counts[:, None]).astype(jnp.float32)
    block_row = jnp.arange(analysis_block_count, dtype=jnp.float32)[:, None]
    row_gap = jnp.take(obs_row, block_lists) - block_row
    col_gap = jnp.take(obs_col, block_lists) - 0.5 * (tile_width - 1)
    tapering = jnp.exp(-0.5 * ((row_gap / LOC_ROWS) ** 2 + (col_gap / LOC_COLS) ** 2))
    weight = active * tapering * jnp.take(precision, block_lists)
    gram_matrix = jnp.einsum('erk,frk->ref', chosen * weight[None], chosen, precision=HIGHEST)
    forcing = jnp.einsum('erk,rk->re', chosen, weight * jnp.take(innovation, block_lists), precision=HIGHEST)
    identity = jnp.eye(sample_realizations, dtype=jnp.float32)
    system = (sample_realizations - 1.0) * identity + gram_matrix
    bounds = sample_realizations - 1.0 + lax.optimization_barrier(jnp.max(lax.optimization_barrier(jnp.sum(jnp.abs(gram_matrix), axis=2)), axis=1))
    upper_iter = system / bounds[:, None, None]
    lower_iter = jnp.broadcast_to(identity, system.shape)
    for iteration in range(NS_ITERS):
        factor = 1.5 * identity - 0.5 * jnp.einsum('rij,rjk->rik', lower_iter, upper_iter, precision=HIGHEST)
        upper_iter = jnp.einsum('rij,rjk->rik', upper_iter, factor, precision=HIGHEST)
        lower_iter = jnp.einsum('rij,rjk->rik', factor, lower_iter, precision=HIGHEST)
    inv_root = lower_iter / jnp.sqrt(bounds)[:, None, None]
    half_shift = jnp.einsum('rij,rj->ri', inv_root, forcing, precision=HIGHEST)
    mean_shift = jnp.einsum('rij,rj->ri', inv_root, half_shift, precision=HIGHEST)
    weights = jnp.sqrt(sample_realizations - 1.0) * inv_root + mean_shift[:, :, None]
    fields = mesh_patch.astype(jnp.float32)
    centre = lax.optimization_barrier(jnp.mean(fields, axis=0))
    anomalies = fields - centre
    updated = centre + jnp.einsum('kvrc,rkm->mvrc', anomalies, weights, precision=HIGHEST)
    return updated.astype(jnp.bfloat16)

def realization_predict(sample_states, wind_cfl_ratios):
    present_states = sample_states.astype(jnp.float32)
    diffusion = jnp.array(KAPPA, jnp.float32).reshape(2, 1, 1)
    for section_index in range(SECTIONS):
        padded = jnp.pad(present_states, ((0, 0), (1, 1), (0, 0)))
        present_states = advance(padded, wind_cfl_ratios[0], wind_cfl_ratios[1], diffusion)
    return present_states.astype(jnp.bfloat16)

def reference(prior_sample_states, wind_cfl_ratios, obs_cell, obs_value, obs_precision, neighbours, obs_counts):
    predict_advance = lax.map(lambda sample_states: realization_predict(sample_states, wind_cfl_ratios), prior_sample_states)
    sample_realizations = prior_sample_states.shape[0]
    quantity_leading = predict_advance[:, 0].reshape(sample_realizations, MESH_HEIGHT * MESH_WIDTH)
    cells = obs_cell.reshape(N_LAT, N_MEM, OBS_DEV)
    row_local = cells // PATCH_WIDTH
    col_local = cells % PATCH_WIDTH
    band_ids = jnp.arange(N_LAT, dtype=jnp.int32)[:, None, None]
    tile_ids = jnp.arange(N_MEM, dtype=jnp.int32)[None, :, None]
    flat_index = ((band_ids * ZONE_HEIGHT + row_local) * MESH_WIDTH + tile_ids * PATCH_WIDTH + col_local).astype(jnp.int32)
    sampled = jnp.take(quantity_leading, flat_index.reshape(-1), axis=1).astype(jnp.float32)
    sampled = jnp.transpose(sampled.reshape(sample_realizations, N_LAT, N_MEM, OBS_DEV), (1, 2, 0, 3))
    meta = jnp.stack([obs_value.reshape(N_LAT, N_MEM, OBS_DEV), obs_precision.reshape(N_LAT, N_MEM, OBS_DEV), row_local.astype(jnp.float32), col_local.astype(jnp.float32)], axis=2)
    combined = jnp.concatenate([sampled, meta], axis=2)
    padded = jnp.pad(combined, ((1, 1), (1, 1), (0, 0), (0, 0)))
    depth = sample_realizations + 4

    def fetch(zonal_strip, mesh_patch):
        return lax.dynamic_slice(padded, index_tuple(zonal_strip, mesh_patch, 0, 0), (1, 1, depth, OBS_DEV))[0, 0]

    def one_tile(index):
        zonal_strip = (index // N_MEM).astype(jnp.int32)
        mesh_patch = (index % N_MEM).astype(jnp.int32)
        pieces = [place_piece(fetch(zonal_strip + 1, mesh_patch + 1), sample_realizations, 0.0, 0.0), place_piece(fetch(zonal_strip, mesh_patch + 1), sample_realizations, -float(ZONE_HEIGHT), 0.0), place_piece(fetch(zonal_strip + 2, mesh_patch + 1), sample_realizations, float(ZONE_HEIGHT), 0.0), place_piece(fetch(zonal_strip + 1, mesh_patch), sample_realizations, 0.0, -float(PATCH_WIDTH)), place_piece(fetch(zonal_strip + 1, mesh_patch + 2), sample_realizations, 0.0, float(PATCH_WIDTH))]
        extended = jnp.concatenate(pieces, axis=1)
        states_by_patch = lax.dynamic_slice(predict_advance, index_tuple(0, 0, zonal_strip * ZONE_HEIGHT, mesh_patch * PATCH_WIDTH), (sample_realizations, 2, ZONE_HEIGHT, PATCH_WIDTH))
        block_lists = lax.dynamic_slice(neighbours, index_tuple(zonal_strip * ZONE_HEIGHT, mesh_patch, 0), (ZONE_HEIGHT, 1, KNB))[:, 0]
        block_counts = lax.dynamic_slice(obs_counts, index_tuple(zonal_strip * ZONE_HEIGHT, mesh_patch), (ZONE_HEIGHT, 1))[:, 0]
        return analyze(states_by_patch, extended, block_lists, block_counts)
    results = lax.map(one_tile, jnp.arange(N_LAT * N_MEM, dtype=jnp.int32))
    results = results.reshape(N_LAT, N_MEM, sample_realizations, 2, ZONE_HEIGHT, PATCH_WIDTH)
    return jnp.transpose(results, (2, 3, 0, 4, 1, 5)).reshape(sample_realizations, 2, MESH_HEIGHT, MESH_WIDTH)
```

```python
import functools
import math

import jax
import jax.numpy as jnp
from jax import lax
from jax.experimental import pallas as pl
from jax.experimental.pallas import tpu as pltpu
from jax.sharding import PartitionSpec as P

W = 128
SECTIONS = 4
NS_ITERS = 6
LOC_ROWS = 2
LOC_COLS = 64
KAPPA = (0.025, 0.0125)
MESH = pl.DeviceIdType.MESH


def matmul(a, b, contract=((1,), (0,))):
    return lax.dot_general(a, b, (contract, ((), ())), preferred_element_type=jnp.float32)


def halves(x):
    high = x.astype(jnp.bfloat16)
    return high, (x - high.astype(jnp.float32)).astype(jnp.bfloat16)


def hp(a, b, contract=((1,), (0,))):
    a_high, a_low = halves(a)
    b_high, b_low = halves(b)
    return matmul(a_high, b_high, contract) + (
        matmul(a_high, b_low, contract) + matmul(a_low, b_high, contract)
    )


def tree(terms):
    while len(terms) > 1:
        terms = [terms[i] + terms[i + 1] for i in range(0, len(terms), 2)]
    return terms[0]


def columns_of(pair, picks):
    return [[jnp.take_along_axis(x, pick, axis=1, mode="promise_in_bounds") for pick in picks] for x in pair]


def product(columns, pair):
    spread_rows = [jnp.broadcast_to(pair[k // 8][k % 8 : k % 8 + 1], (8, W)) for k in range(16)]
    return [tree([a * b for a, b in zip(half, spread_rows)]) for half in columns]


def kernel(
    n_mem, n_lat,
    prior_hbm, wind_hbm, cell_hbm, value_hbm, prec_hbm, nb_hbm, cnt_hbm,
    out_ref,
    prior, wind, cells, value, prec, nb, cnt, meta, packed, tiles, beside, moved, laid,
    load_sem, halo_send, halo_recv, meta_send, meta_recv, tile_send, tile_recv, back_send, back_recv, ready,
):
    f32, bf16, i32 = jnp.float32, jnp.bfloat16, jnp.int32
    u = lax.axis_index("mem")
    t = lax.axis_index("lat")
    members, _, rows, cols = prior_hbm.shape
    slots = nb_hbm.shape[2]
    n_obs = cell_hbm.shape[1]
    ens = members * n_mem
    big = ens * rows
    half = members * rows

    lat_up, lat_down, mem_up, mem_down = t + 1, t - 1, u + 1, u - 1
    above, below = t < n_lat - 1, t > 0
    east_of, west_of = u < n_mem - 1, u > 0
    lats = 1 + above.astype(i32) + below.astype(i32)

    def partner(k):
        up = k + (k >= u).astype(i32)
        k = n_mem - 1 - k
        return jnp.where(2 * u >= n_mem, up, k - (k <= u).astype(i32))

    def signal(sem, mem, lat):
        pl.semaphore_signal(sem, inc=1, device_id={"mem": mem, "lat": lat}, device_id_type=MESH)

    def signal_lats(sem, mem):
        signal(sem, mem, t)
        pl.when(above)(lambda: signal(sem, mem, lat_up))
        pl.when(below)(lambda: signal(sem, mem, lat_down))

    loads = [
        pltpu.make_async_copy(src, dst, load_sem.at[i])
        for i, (src, dst) in enumerate((
            (prior_hbm, prior.at[1]), (wind_hbm, wind.at[1]), (cell_hbm, cells), (value_hbm, value),
            (prec_hbm, prec), (nb_hbm, nb), (cnt_hbm, cnt),
        ))
    ]
    for load in loads:
        load.start()

    barrier = pltpu.get_barrier_semaphore()
    pl.when(above)(lambda: signal(barrier, u, lat_up))
    pl.when(below)(lambda: signal(barrier, u, lat_down))

    def greet(d, carry):
        signal_lats(barrier, n_mem - 1 - d)
        return carry

    lax.fori_loop(0, n_mem - 1 - u, greet, 0)
    pl.semaphore_wait(barrier, lats * (u + 1) - 1)
    for load in loads[:2]:
        load.wait()

    def halo_copies(side, lat):
        return [
            pltpu.make_async_remote_copy(
                src_ref=src, dst_ref=dst.at[2 * side],
                send_sem=halo_send.at[side, kind], recv_sem=halo_recv.at[side, kind],
                device_id={"mem": u, "lat": lat}, device_id_type=MESH,
            )
            for kind, (src, dst) in enumerate(((prior.at[1], prior), (wind.at[1], wind)))
        ]

    def each(copies, act):
        for copy in copies:
            getattr(copy, act)()

    up_halo, down_halo = halo_copies(0, lat_up), halo_copies(1, lat_down)
    pl.when(above)(lambda: each(up_halo, "start"))
    pl.when(below)(lambda: each(down_halo, "start"))

    def answer(mem, carry):
        signal_lats(ready, mem)
        return carry

    lax.fori_loop(0, u, answer, 0)

    for load in loads[2:]:
        load.wait()
    meta[0, 0:1, :] = cells[...].astype(f32)
    meta[0, 1:2, :] = value[...]
    meta[0, 2:3, :] = prec[...]
    meta[0, 3:8, :] = jnp.zeros((5, n_obs), f32)
    metas = [
        pltpu.make_async_remote_copy(
            src_ref=meta.at[0], dst_ref=meta.at[slot + 1],
            send_sem=meta_send.at[slot], recv_sem=meta_recv.at[slot],
            device_id={"mem": mem, "lat": lat}, device_id_type=MESH,
        )
        for slot, (mem, lat) in enumerate(((u, lat_up), (u, lat_down), (mem_up, t), (mem_down, t)))
    ]
    meta_to = (above, below, east_of, west_of)
    meta_from = (below, above, west_of, east_of)

    def meta_zero(slot):
        meta[slot + 1] = jnp.zeros((8, n_obs), f32)

    for slot in (0, 1, 3):
        pl.when(meta_to[slot])(metas[slot].start)
    for slot in range(4):
        pl.when(jnp.logical_not(meta_from[slot]))(functools.partial(meta_zero, slot))

    n_ext = 5 * n_obs
    n_hi = n_ext // W
    listed = jnp.concatenate([nb[r] for r in range(rows)], axis=1)
    counts = jnp.concatenate(
        [jnp.broadcast_to(cnt[:, r : r + 1], (1, slots)) for r in range(rows)], axis=1
    )
    position = lax.broadcasted_iota(i32, (1, rows * slots), 1)
    hi = lax.shift_right_logical(listed, 7)
    lo = lax.bitwise_and(listed, W - 1)
    hi = jnp.where(lax.bitwise_and(position, slots - 1) < counts, hi, n_hi + 8)
    sub = lax.broadcasted_iota(i32, (8 * n_hi, rows * slots), 0)
    owner = position // slots
    key = hi * 8 + owner
    left = (sub == key).astype(f32) + (sub == key + rows).astype(f32)
    right = (lax.broadcasted_iota(i32, (W, rows * slots), 0) == lo).astype(f32)
    member = matmul(left.astype(bf16), right.astype(bf16), ((1,), (1,)))
    member = jnp.concatenate([member[8 * h : 8 * h + 8] for h in range(n_hi)], axis=1)

    pl.when(below)(lambda: each(up_halo, "wait_recv"))
    pl.when(above)(lambda: each(down_halo, "wait_recv"))
    wide = 4 * rows
    row_id = lax.broadcasted_iota(i32, (wide, cols), 0)
    col_id = lax.broadcasted_iota(i32, (wide, cols), 1)
    first_row = jnp.where(t == 0, rows, 0)
    last_row = jnp.where(t == n_lat - 1, 2 * rows, 3 * rows)
    inside = (row_id >= first_row) & (row_id < last_row)

    def band(parts):
        return jnp.concatenate(list(parts) + [jnp.zeros((rows, cols), f32)], axis=0)

    east = band(wind[s, 0] for s in range(3))
    north = band(wind[s, 1] for s in range(3))
    east_pos, east_neg = jnp.maximum(east, 0.0), jnp.minimum(east, 0.0)
    north_pos, north_neg = jnp.maximum(north, 0.0), jnp.minimum(north, 0.0)
    fields = []
    for var in range(2):
        kappa = KAPPA[var]
        keep = jnp.where(inside, 1.0 - (east_pos - east_neg + north_pos - north_neg) - 4.0 * kappa, 0.0)
        from_west = jnp.where(inside & (col_id > 0), east_pos + kappa, 0.0)
        from_east = jnp.where(inside & (col_id < cols - 1), kappa - east_neg, 0.0)
        from_south = jnp.where(inside, north_pos + kappa, 0.0)
        from_north = jnp.where(inside, kappa - north_neg, 0.0)
        own = []
        for j in range(members):
            q = jnp.where(inside, band(prior[s, j, var].astype(f32) for s in range(3)), 0.0)
            for _ in range(SECTIONS):
                q = (
                    keep * q
                    + from_west * pltpu.roll(q, 1, 1)
                    + from_east * pltpu.roll(q, cols - 1, 1)
                    + from_south * pltpu.roll(q, 1, 0)
                    + from_north * pltpu.roll(q, wide - 1, 0)
                )
            own.append(q[rows : 2 * rows])
        fields.append(jnp.concatenate(own, axis=0).astype(bf16))
    for k in range(n_mem):
        for place, (var, tile) in enumerate(((0, (k - 1) % n_mem), (0, k), (0, (k + 1) % n_mem), (1, k))):
            packed[k, :, place * W : (place + 1) * W] = fields[var][:, tile * W : (tile + 1) * W]

    def beside_copy(mem, side, lat):
        return pltpu.make_async_remote_copy(
            src_ref=packed.at[mem, :, pl.ds(W, W)], dst_ref=beside.at[side, u],
            send_sem=tile_send.at[1 + side, mem], recv_sem=tile_recv.at[1 + side, u],
            device_id={"mem": mem, "lat": lat}, device_id_type=MESH,
        )

    def tile_copy(mem):
        return pltpu.make_async_remote_copy(
            src_ref=packed.at[mem], dst_ref=tiles.at[u],
            send_sem=tile_send.at[0, mem], recv_sem=tile_recv.at[0, u],
            device_id={"mem": mem, "lat": t}, device_id_type=MESH,
        )

    def beside_both(mem, act):
        pl.when(above)(lambda: getattr(beside_copy(mem, 0, lat_up), act)())
        pl.when(below)(lambda: getattr(beside_copy(mem, 1, lat_down), act)())

    pl.when(east_of)(lambda: pl.semaphore_wait(ready, lats * (n_mem - 1 - u)))
    pl.when(east_of)(metas[2].start)

    def send_tiles(k, carry):
        mem = partner(k)
        tile_copy(mem).start()
        beside_both(mem, "start")
        return carry

    lax.fori_loop(0, n_mem - 1, send_tiles, 0)
    beside_both(u, "start")
    own_tile = pltpu.make_async_copy(packed.at[u], tiles.at[u], tile_recv.at[0, u])
    own_tile.start()

    def beside_zero(side):
        beside[side] = jnp.zeros(beside.shape[1:], bf16)

    pl.when(jnp.logical_not(below))(lambda: beside_zero(0))
    pl.when(jnp.logical_not(above))(lambda: beside_zero(1))

    for slot in range(4):
        pl.when(meta_from[slot])(metas[slot].wait_recv)
    cell = jnp.concatenate([meta[i, 0:1, :] for i in range(5)], axis=1)
    observed = jnp.concatenate([meta[i, 1:2, :] for i in range(5)], axis=1)
    valid = (None,) + meta_from
    precision = jnp.concatenate(
        [meta[0, 2:3, :]] + [jnp.where(valid[i], meta[i, 2:3, :], 0.0) for i in range(1, 5)], axis=1
    )
    cell_row = jnp.floor(cell * (1.0 / W))
    cell_col = cell - W * cell_row

    def spread_out(shifts):
        return jnp.concatenate([jnp.full((1, n_obs), s, f32) for s in shifts], axis=1)

    ext_row = cell_row + spread_out((0.0, -float(rows), float(rows), 0.0, 0.0))
    ext_col = cell_col + spread_out((0.0, 0.0, 0.0, -float(W), float(W)))
    block = lax.bitwise_and(lax.broadcasted_iota(i32, (8, n_ext), 0), rows - 1).astype(f32)
    row_gap = (ext_row - block) * (1.0 / LOC_ROWS)
    col_gap = (ext_col - 0.5 * (W - 1)) * (1.0 / LOC_COLS)
    weight = member * jnp.exp(-0.5 * (row_gap * row_gap + col_gap * col_gap)) * precision
    select = (lax.broadcasted_iota(i32, (W, n_ext), 0).astype(f32) == cell_col).astype(f32).astype(bf16)
    at_row = jnp.where(block == cell_row, 1.0, 0.0)
    compact = ens == 16 and rows == 4
    if compact:
        lane, sub = lax.broadcasted_iota(i32, (8, W), 1), lax.broadcasted_iota(i32, (8, W), 0)
        lane_block = lax.bitwise_and(lane // ens, rows - 1)
        picks = [lane - lax.bitwise_and(lane, ens - 1) + k for k in range(ens)]
        unit = [(lax.bitwise_and(lane, ens - 1) == sub + 8 * h).astype(f32) for h in range(2)]
        in_block = [lane_block == r for r in range(rows)]
        of_row = [lax.bitwise_and(sub, rows - 1) == r for r in range(rows)]
        mine = lane_block == lax.bitwise_and(sub, rows - 1)
        in_row = [cell_row == float(r) for r in range(rows - 1)]
    else:
        ids0 = lax.broadcasted_iota(i32, (big, big), 0)
        ids1 = lax.broadcasted_iota(i32, (big, big), 1)
        same_member = (ids0 // rows == ids1 // rows).astype(f32).astype(bf16)
        same_block = lax.bitwise_and(ids0, rows - 1) == lax.bitwise_and(ids1, rows - 1)
        identity = (ids0 == ids1).astype(f32)

    own_tile.wait()

    def wait_tiles(k, carry):
        mem = partner(k)
        pltpu.make_async_copy(packed.at[0], tiles.at[mem], tile_recv.at[0, mem]).wait()
        return carry

    def wait_beside(side):
        def wait_one(mem, carry):
            pltpu.make_async_copy(
                packed.at[0, :, pl.ds(W, W)], beside.at[side, mem], tile_recv.at[1 + side, mem]
            ).wait()
            return carry

        lax.fori_loop(0, n_mem, wait_one, 0)

    lax.fori_loop(0, n_mem - 1, wait_tiles, 0)
    pl.when(below)(lambda: wait_beside(0))
    pl.when(above)(lambda: wait_beside(1))

    def flat(x):
        return x.reshape(big, x.shape[-1])

    if compact:
        for at in range(4):
            laid[at] = flat(tiles[:, :, at * W : (at + 1) * W]).astype(f32)
        for side in range(2):
            laid[4 + side] = flat(beside[side]).astype(f32)
        by_row = [[laid[at, pl.ds(r, ens, stride=rows), :] for at in range(6)] for r in range(rows)]
        obs = []
        for i, at in enumerate((1, 4, 5, 0, 2)):
            x = jnp.concatenate([q[at] for q in by_row], axis=0)
            here_obs = slice(i * n_obs, (i + 1) * n_obs)
            x = matmul(x.astype(bf16), select[:, here_obs])
            best = x[(rows - 1) * ens : rows * ens]
            for r in range(rows - 1):
                best = jnp.where(in_row[r][:, here_obs], x[r * ens : (r + 1) * ens], best)
            obs.append(best)
        obs = jnp.concatenate(obs, axis=1)
        obs_mean = jnp.sum(obs[0:8] + obs[8:16], axis=0, keepdims=True) * (1.0 / ens)
        spread = obs - obs_mean
        innovation = jnp.broadcast_to(observed - obs_mean, (8, n_ext))
        w_high, w_low = halves(jnp.concatenate([spread * weight[r : r + 1] for r in range(rows)], axis=0))
        s_high, s_low = halves(jnp.concatenate([spread] * 8 + [innovation], axis=0))
        across = ((1,), (1,))
        two = matmul(jnp.concatenate([w_high, w_low], axis=0), s_high, across)
        sums = two[0:big] + (two[big : 2 * big] + matmul(w_high, s_low, across))
        forcing = jnp.broadcast_to(sums[:, W : W + 1], (big, W))
        gram = []
        for h in range(2):
            part = sums[8 * h : 8 * h + 8, 0:W]
            for r in range(1, rows):
                part = jnp.where(in_block[r], sums[r * ens + 8 * h : r * ens + 8 * h + 8, 0:W], part)
            gram.append(part)

        anomalies, centre = [], jnp.zeros((8, 2 * W), f32)
        for r in range(rows):
            x = jnp.concatenate([by_row[r][1], by_row[r][3]], axis=1)
            mean = jnp.sum(x[0:8] + x[8:16], axis=0, keepdims=True) * (1.0 / ens)
            anomalies.append(x - mean)
            centre = jnp.where(jnp.concatenate([of_row[r]] * 2, axis=1), jnp.broadcast_to(mean, (8, 2 * W)), centre)
        e_high, e_low = halves(jnp.concatenate([jnp.concatenate(anomalies, axis=0), forcing], axis=1))
        extra = jnp.concatenate([e_high, e_low], axis=0)

        def combined(p, x, q, y):
            return [p * a + q * b for a, b in zip(x, y)]

        columns = columns_of(gram, picks)
        row_sums = [tree([jnp.abs(c) for c in half]) for half in columns]
        top = jnp.max(jnp.maximum(row_sums[0], row_sums[1]), axis=0, keepdims=True)
        bound = (ens - 1.0) + jnp.broadcast_to(top, (8, W))
        scale = 1.0 / bound
        end_scale = 1.0 / jnp.sqrt(bound)

        def system_times(x):
            return [scale * y for y in combined(ens - 1.0, x, 1.0, product(columns, x))]

        joint = [scale * y for y in combined(ens - 1.0, unit, 1.0, gram)]
        lower = combined(1.5, unit, -0.5, joint)
        half_way = combined(1.5, joint, -0.5, system_times(joint))
        joint = combined(1.5, half_way, -0.5, system_times(half_way))
        for step in range(1, NS_ITERS - 1):
            columns = columns_of(joint, picks)
            half_way = combined(1.5, joint, -0.5, product(columns, joint))
            lower = combined(1.5, lower, -0.5, product(columns, lower))
            joint = combined(1.5, half_way, -0.5, product(columns, half_way))
        root = combined(1.5, lower, -0.5, product(columns_of(lower, picks), joint))
        root = [x * end_scale for x in root]
        root_rows = []
        for v in range(big // 8):
            side, at = root[v // 4], (2 * v) % 8
            pair = jnp.where(
                sub < rows,
                jnp.broadcast_to(side[at : at + 1], (8, W)),
                jnp.broadcast_to(side[at + 1 : at + 2], (8, W)),
            )
            root_rows.append(jnp.where(mine, pair, 0.0))
        r_high, r_low = halves(jnp.concatenate(root_rows, axis=0))
        two = matmul(jnp.concatenate([r_high, r_low], axis=0), extra)
        rooted = two[0:big] + two[big : 2 * big]
        turned, half_shift = rooted[:, 0 : 2 * W], rooted[:, 2 * W : 3 * W]
        half_shift = jnp.concatenate([half_shift, half_shift], axis=1)
    else:
        states = tiles[...].astype(f32)

        sources = (
            states[:, :, W : 2 * W], beside[0].astype(f32), beside[1].astype(f32),
            states[:, :, 0:W], states[:, :, 2 * W : 3 * W],
        )
        picked = jnp.concatenate(
            [
                matmul(flat(x).astype(bf16), select[:, i * n_obs : (i + 1) * n_obs])
                for i, x in enumerate(sources)
            ],
            axis=1,
        )
        picked = picked.reshape(n_mem, 8, n_ext) * at_row[None]
        obs = matmul(same_member, flat(picked).astype(bf16))
        obs3 = obs.reshape(n_mem, 8, n_ext)
        folded = jnp.sum(obs3, axis=0)
        obs_mean = jnp.sum(folded, axis=0, keepdims=True) * (1.0 / big)
        spread = obs - obs_mean
        innovation = observed - obs_mean
        weighted = flat(spread.reshape(n_mem, 8, n_ext) * weight[None])
        gram = jnp.where(same_block, hp(weighted, spread, ((1,), (1,))), 0.0)
        forcing = jnp.sum(weighted * innovation, axis=1, keepdims=True)

        fields3 = jnp.concatenate([states[:, :, W : 2 * W], states[:, :, 3 * W : 4 * W]], axis=2)
        total = jnp.sum(fields3, axis=0)
        centre = (total + pltpu.roll(total, rows, 0)) * (1.0 / ens)
        anomalies = flat(fields3 - centre[None])
        extra = jnp.concatenate([anomalies, jnp.broadcast_to(forcing, (big, W))], axis=1)

        row_sums = jnp.broadcast_to(jnp.sum(jnp.abs(gram), axis=1, keepdims=True), (big, W))
        top = jnp.max(row_sums.reshape(n_mem, 8, W), axis=0)
        top = jnp.maximum(top, pltpu.roll(top, rows, 0))
        bound = (ens - 1.0) + jnp.broadcast_to(top[None], (n_mem, 8, W)).reshape(big, W)[:, 0:1]
        upper = ((ens - 1.0) * identity + gram) / bound
        factor = 1.5 * identity - 0.5 * upper
        lower = factor
        upper = hp(upper, factor)
        for step in range(1, NS_ITERS):
            factor = 1.5 * identity - 0.5 * hp(lower, upper)
            if step < NS_ITERS - 1:
                upper = hp(upper, factor)
                lower = hp(factor, lower)
        rooted = hp(factor, hp(lower, extra)) / jnp.sqrt(bound)
        turned, half_shift = rooted[:, 0 : 2 * W], rooted[:, 2 * W : 2 * W + 1]
    shift = jnp.sum((turned * half_shift).reshape(n_mem, 8, 2 * W), axis=0)
    base = centre + shift + pltpu.roll(shift, rows, 0)
    updated = (math.sqrt(ens - 1.0) * turned).reshape(n_mem, 8, 2 * W) + base[None]
    for j in range(members):
        for var in range(2):
            moved[:, j, var] = updated[:, j * rows : (j + 1) * rows, var * W : (var + 1) * W].astype(bf16)

    def here(k):
        return out_ref.at[:, :, :, pl.ds(pl.multiple_of(k * W, W), W)]

    def back_copy(mem):
        return pltpu.make_async_remote_copy(
            src_ref=moved.at[mem], dst_ref=here(u),
            send_sem=back_send.at[mem], recv_sem=back_recv.at[u],
            device_id={"mem": mem, "lat": t}, device_id_type=MESH,
        )

    own_back = pltpu.make_async_copy(moved.at[u], here(u), back_recv.at[u])

    def send_back(k, carry):
        back_copy(partner(k)).start()
        return carry

    lax.fori_loop(0, n_mem - 1, send_back, 0)
    own_back.start()

    def drain(k, carry):
        mem = partner(k)
        tile_copy(mem).wait_send()
        beside_both(mem, "wait_send")
        return carry

    lax.fori_loop(0, n_mem - 1, drain, 0)
    beside_both(u, "wait_send")
    pl.when(above)(lambda: each(up_halo, "wait_send"))
    pl.when(below)(lambda: each(down_halo, "wait_send"))
    for slot in range(4):
        pl.when(meta_to[slot])(metas[slot].wait_send)
    own_back.wait()

    def wait_back(k, carry):
        mem = partner(k)
        back_copy(mem).wait_send()
        pltpu.make_async_copy(moved.at[mem], here(mem), back_recv.at[mem]).wait()
        return carry

    lax.fori_loop(0, n_mem - 1, wait_back, 0)


def on_device(n_mem, n_lat, *args):
    prior, wind, cell, value, prec, nb, cnt = args
    cnt = cnt.T
    members, _, rows, cols = prior.shape
    n_obs = cell.shape[1]
    f32, bf16, i32 = jnp.float32, jnp.bfloat16, jnp.int32
    dma = pltpu.SemaphoreType.DMA
    return pl.pallas_call(
        functools.partial(kernel, n_mem, n_lat),
        out_shape=pltpu.VMEM(prior.shape, bf16),
        in_specs=[pl.BlockSpec(memory_space=pl.ANY)] * 7,
        out_specs=pl.BlockSpec(memory_space=pltpu.VMEM),
        scratch_shapes=[
            pltpu.VMEM((3,) + prior.shape, bf16),
            pltpu.VMEM((3,) + wind.shape, f32),
            pltpu.VMEM(cell.shape, i32),
            pltpu.VMEM(value.shape, f32),
            pltpu.VMEM(prec.shape, f32),
            pltpu.VMEM(nb.shape, i32),
            pltpu.VMEM(cnt.shape, i32),
            pltpu.VMEM((5, 8, n_obs), f32),
            pltpu.VMEM((n_mem, members * rows, 4 * W), bf16),
            pltpu.VMEM((n_mem, members * rows, 4 * W), bf16),
            pltpu.VMEM((2, n_mem, members * rows, W), bf16),
            pltpu.VMEM((n_mem, members, 2, rows, W), bf16),
            pltpu.VMEM((6, n_mem * members * rows, W), f32),
            dma((7,)), dma((2, 2)), dma((2, 2)), dma((4,)), dma((4,)),
            dma((3, n_mem)), dma((3, n_mem)), dma((n_mem,)), dma((n_mem,)), pltpu.SemaphoreType.REGULAR,
        ],
        compiler_params=pltpu.CompilerParams(collective_id=0, has_side_effects=True),
    )(prior, wind, cell, value, prec, nb, cnt)


def solution(mesh):
    placed = (
        P("mem", None, "lat", None),
        P(None, "lat", None),
        P("lat", "mem"),
        P("lat", "mem"),
        P("lat", "mem"),
        P("lat", "mem", None),
        P("lat", "mem"),
    )
    return jax.shard_map(
        functools.partial(on_device, mesh.shape["mem"], mesh.shape["lat"]),
        mesh=mesh,
        in_specs=placed,
        out_specs=P("mem", None, "lat", None),
        check_vma=False,
    )
```

```python
import functools
import math

import jax
import jax.numpy as jnp
from jax import lax
from jax.experimental import pallas as pl
from jax.experimental.pallas import tpu as pltpu
from jax.sharding import PartitionSpec as P

W = 128
SECTIONS = 4
NS_ITERS = 6
LOC_ROWS = 2
LOC_COLS = 64
KAPPA = (0.025, 0.0125)
MESH = pl.DeviceIdType.MESH


def matmul(a, b, contract=((1,), (0,))):
    return lax.dot_general(a, b, (contract, ((), ())), preferred_element_type=jnp.float32)


def halves(x):
    high = x.astype(jnp.bfloat16)
    return high, (x - high.astype(jnp.float32)).astype(jnp.bfloat16)


def hp(a, b, contract=((1,), (0,))):
    a_high, a_low = halves(a)
    b_high, b_low = halves(b)
    return matmul(a_high, b_high, contract) + (
        matmul(a_high, b_low, contract) + matmul(a_low, b_high, contract)
    )


def kernel(
    n_mem, n_lat,
    prior_hbm, wind_hbm, cell_hbm, value_hbm, prec_hbm, nb_hbm, cnt_hbm,
    out_ref,
    prior, wind, cells, value, prec, nb, cnt, meta, packed, tiles, beside, moved,
    load_sem, halo_send, halo_recv, meta_send, meta_recv, tile_send, tile_recv, back_send, back_recv, ready,
):
    f32, bf16, i32 = jnp.float32, jnp.bfloat16, jnp.int32
    u = lax.axis_index("mem")
    t = lax.axis_index("lat")
    members, _, rows, cols = prior_hbm.shape
    slots = nb_hbm.shape[2]
    n_obs = cell_hbm.shape[1]
    ens = members * n_mem
    big = ens * rows
    half = members * rows

    lat_up, lat_down, mem_up, mem_down = t + 1, t - 1, u + 1, u - 1
    above, below = t < n_lat - 1, t > 0
    east_of, west_of = u < n_mem - 1, u > 0
    lats = 1 + above.astype(i32) + below.astype(i32)

    def partner(k):
        up = k + (k >= u).astype(i32)
        k = n_mem - 1 - k
        return jnp.where(2 * u >= n_mem, up, k - (k <= u).astype(i32))

    def signal(sem, mem, lat):
        pl.semaphore_signal(sem, inc=1, device_id={"mem": mem, "lat": lat}, device_id_type=MESH)

    def signal_lats(sem, mem):
        signal(sem, mem, t)
        pl.when(above)(lambda: signal(sem, mem, lat_up))
        pl.when(below)(lambda: signal(sem, mem, lat_down))

    loads = [
        pltpu.make_async_copy(src, dst, load_sem.at[i])
        for i, (src, dst) in enumerate((
            (prior_hbm, prior.at[1]), (wind_hbm, wind.at[1]), (cell_hbm, cells), (value_hbm, value),
            (prec_hbm, prec), (nb_hbm, nb), (cnt_hbm, cnt),
        ))
    ]
    for load in loads:
        load.start()

    barrier = pltpu.get_barrier_semaphore()
    pl.when(above)(lambda: signal(barrier, u, lat_up))
    pl.when(below)(lambda: signal(barrier, u, lat_down))

    def greet(d, carry):
        signal_lats(barrier, n_mem - 1 - d)
        return carry

    lax.fori_loop(0, n_mem - 1 - u, greet, 0)
    pl.semaphore_wait(barrier, lats * (u + 1) - 1)
    for load in loads[:2]:
        load.wait()

    def halo_copies(side, lat):
        return [
            pltpu.make_async_remote_copy(
                src_ref=src, dst_ref=dst.at[2 * side],
                send_sem=halo_send.at[side, kind], recv_sem=halo_recv.at[side, kind],
                device_id={"mem": u, "lat": lat}, device_id_type=MESH,
            )
            for kind, (src, dst) in enumerate(((prior.at[1], prior), (wind.at[1], wind)))
        ]

    def each(copies, act):
        for copy in copies:
            getattr(copy, act)()

    up_halo, down_halo = halo_copies(0, lat_up), halo_copies(1, lat_down)
    pl.when(above)(lambda: each(up_halo, "start"))
    pl.when(below)(lambda: each(down_halo, "start"))

    def answer(mem, carry):
        signal_lats(ready, mem)
        return carry

    lax.fori_loop(0, u, answer, 0)

    for load in loads[2:]:
        load.wait()
    meta[0, 0:1, :] = cells[...].astype(f32)
    meta[0, 1:2, :] = value[...]
    meta[0, 2:3, :] = prec[...]
    meta[0, 3:8, :] = jnp.zeros((5, n_obs), f32)
    metas = [
        pltpu.make_async_remote_copy(
            src_ref=meta.at[0], dst_ref=meta.at[slot + 1],
            send_sem=meta_send.at[slot], recv_sem=meta_recv.at[slot],
            device_id={"mem": mem, "lat": lat}, device_id_type=MESH,
        )
        for slot, (mem, lat) in enumerate(((u, lat_up), (u, lat_down), (mem_up, t), (mem_down, t)))
    ]
    meta_to = (above, below, east_of, west_of)
    meta_from = (below, above, west_of, east_of)

    def meta_zero(slot):
        meta[slot + 1] = jnp.zeros((8, n_obs), f32)

    for slot in (0, 1, 3):
        pl.when(meta_to[slot])(metas[slot].start)
    for slot in range(4):
        pl.when(jnp.logical_not(meta_from[slot]))(functools.partial(meta_zero, slot))

    n_ext = 5 * n_obs
    n_hi = n_ext // W
    listed = jnp.concatenate([nb[r] for r in range(rows)], axis=1)
    counts = jnp.concatenate(
        [jnp.broadcast_to(cnt[:, r : r + 1], (1, slots)) for r in range(rows)], axis=1
    )
    position = lax.broadcasted_iota(i32, (1, rows * slots), 1)
    hi = lax.shift_right_logical(listed, 7)
    lo = lax.bitwise_and(listed, W - 1)
    hi = jnp.where(lax.bitwise_and(position, slots - 1) < counts, hi, n_hi + 8)
    sub = lax.broadcasted_iota(i32, (8 * n_hi, rows * slots), 0)
    owner = position // slots
    key = hi * 8 + owner
    left = (sub == key).astype(f32) + (sub == key + rows).astype(f32)
    right = (lax.broadcasted_iota(i32, (W, rows * slots), 0) == lo).astype(f32)
    member = matmul(left.astype(bf16), right.astype(bf16), ((1,), (1,)))
    member = jnp.concatenate([member[8 * h : 8 * h + 8] for h in range(n_hi)], axis=1)

    pl.when(below)(lambda: each(up_halo, "wait_recv"))
    pl.when(above)(lambda: each(down_halo, "wait_recv"))
    wide = 4 * rows
    row_id = lax.broadcasted_iota(i32, (wide, cols), 0)
    col_id = lax.broadcasted_iota(i32, (wide, cols), 1)
    first_row = jnp.where(t == 0, rows, 0)
    last_row = jnp.where(t == n_lat - 1, 2 * rows, 3 * rows)
    inside = (row_id >= first_row) & (row_id < last_row)

    def band(parts):
        return jnp.concatenate(list(parts) + [jnp.zeros((rows, cols), f32)], axis=0)

    east = band(wind[s, 0] for s in range(3))
    north = band(wind[s, 1] for s in range(3))
    east_pos, east_neg = jnp.maximum(east, 0.0), jnp.minimum(east, 0.0)
    north_pos, north_neg = jnp.maximum(north, 0.0), jnp.minimum(north, 0.0)
    fields = []
    for var in range(2):
        kappa = KAPPA[var]
        keep = jnp.where(inside, 1.0 - (east_pos - east_neg + north_pos - north_neg) - 4.0 * kappa, 0.0)
        from_west = jnp.where(inside & (col_id > 0), east_pos + kappa, 0.0)
        from_east = jnp.where(inside & (col_id < cols - 1), kappa - east_neg, 0.0)
        from_south = jnp.where(inside, north_pos + kappa, 0.0)
        from_north = jnp.where(inside, kappa - north_neg, 0.0)
        own = []
        for j in range(members):
            q = jnp.where(inside, band(prior[s, j, var].astype(f32) for s in range(3)), 0.0)
            for _ in range(SECTIONS):
                q = (
                    keep * q
                    + from_west * pltpu.roll(q, 1, 1)
                    + from_east * pltpu.roll(q, cols - 1, 1)
                    + from_south * pltpu.roll(q, 1, 0)
                    + from_north * pltpu.roll(q, wide - 1, 0)
                )
            own.append(q[rows : 2 * rows])
        fields.append(jnp.concatenate(own, axis=0).astype(bf16))
    for k in range(n_mem):
        for place, (var, tile) in enumerate(((0, (k - 1) % n_mem), (0, k), (0, (k + 1) % n_mem), (1, k))):
            packed[k, :, place * W : (place + 1) * W] = fields[var][:, tile * W : (tile + 1) * W]

    def beside_copy(mem, side, lat):
        return pltpu.make_async_remote_copy(
            src_ref=packed.at[mem, :, pl.ds(W, W)], dst_ref=beside.at[side, u],
            send_sem=tile_send.at[1 + side, mem], recv_sem=tile_recv.at[1 + side, u],
            device_id={"mem": mem, "lat": lat}, device_id_type=MESH,
        )

    def tile_copy(mem):
        return pltpu.make_async_remote_copy(
            src_ref=packed.at[mem], dst_ref=tiles.at[u],
            send_sem=tile_send.at[0, mem], recv_sem=tile_recv.at[0, u],
            device_id={"mem": mem, "lat": t}, device_id_type=MESH,
        )

    def beside_both(mem, act):
        pl.when(above)(lambda: getattr(beside_copy(mem, 0, lat_up), act)())
        pl.when(below)(lambda: getattr(beside_copy(mem, 1, lat_down), act)())

    pl.when(east_of)(lambda: pl.semaphore_wait(ready, lats * (n_mem - 1 - u)))
    pl.when(east_of)(metas[2].start)

    def send_tiles(k, carry):
        mem = partner(k)
        tile_copy(mem).start()
        beside_both(mem, "start")
        return carry

    lax.fori_loop(0, n_mem - 1, send_tiles, 0)
    beside_both(u, "start")
    own_tile = pltpu.make_async_copy(packed.at[u], tiles.at[u], tile_recv.at[0, u])
    own_tile.start()

    def beside_zero(side):
        beside[side] = jnp.zeros(beside.shape[1:], bf16)

    pl.when(jnp.logical_not(below))(lambda: beside_zero(0))
    pl.when(jnp.logical_not(above))(lambda: beside_zero(1))

    for slot in range(4):
        pl.when(meta_from[slot])(metas[slot].wait_recv)
    cell = jnp.concatenate([meta[i, 0:1, :] for i in range(5)], axis=1)
    observed = jnp.concatenate([meta[i, 1:2, :] for i in range(5)], axis=1)
    valid = (None,) + meta_from
    precision = jnp.concatenate(
        [meta[0, 2:3, :]] + [jnp.where(valid[i], meta[i, 2:3, :], 0.0) for i in range(1, 5)], axis=1
    )
    cell_row = jnp.floor(cell * (1.0 / W))
    cell_col = cell - W * cell_row

    def spread_out(shifts):
        return jnp.concatenate([jnp.full((1, n_obs), s, f32) for s in shifts], axis=1)

    ext_row = cell_row + spread_out((0.0, -float(rows), float(rows), 0.0, 0.0))
    ext_col = cell_col + spread_out((0.0, 0.0, 0.0, -float(W), float(W)))
    block = lax.bitwise_and(lax.broadcasted_iota(i32, (8, n_ext), 0), rows - 1).astype(f32)
    row_gap = (ext_row - block) * (1.0 / LOC_ROWS)
    col_gap = (ext_col - 0.5 * (W - 1)) * (1.0 / LOC_COLS)
    weight = member * jnp.exp(-0.5 * (row_gap * row_gap + col_gap * col_gap)) * precision
    select = (lax.broadcasted_iota(i32, (W, n_ext), 0).astype(f32) == cell_col).astype(f32).astype(bf16)
    at_row = jnp.where(block == cell_row, 1.0, 0.0)
    ids0 = lax.broadcasted_iota(i32, (big, big), 0)
    ids1 = lax.broadcasted_iota(i32, (big, big), 1)
    same_member = (ids0 // rows == ids1 // rows).astype(f32).astype(bf16)
    same_block = lax.bitwise_and(ids0, rows - 1) == lax.bitwise_and(ids1, rows - 1)
    identity = (ids0 == ids1).astype(f32)

    own_tile.wait()

    def wait_tiles(k, carry):
        mem = partner(k)
        pltpu.make_async_copy(packed.at[0], tiles.at[mem], tile_recv.at[0, mem]).wait()
        return carry

    def wait_beside(side):
        def wait_one(mem, carry):
            pltpu.make_async_copy(
                packed.at[0, :, pl.ds(W, W)], beside.at[side, mem], tile_recv.at[1 + side, mem]
            ).wait()
            return carry

        lax.fori_loop(0, n_mem, wait_one, 0)

    lax.fori_loop(0, n_mem - 1, wait_tiles, 0)
    pl.when(below)(lambda: wait_beside(0))
    pl.when(above)(lambda: wait_beside(1))

    states = tiles[...].astype(f32)

    def flat(x):
        return x.reshape(big, x.shape[-1])

    sources = (
        states[:, :, W : 2 * W], beside[0].astype(f32), beside[1].astype(f32),
        states[:, :, 0:W], states[:, :, 2 * W : 3 * W],
    )
    picked = jnp.concatenate(
        [
            matmul(flat(x).astype(bf16), select[:, i * n_obs : (i + 1) * n_obs])
            for i, x in enumerate(sources)
        ],
        axis=1,
    )
    picked = picked.reshape(n_mem, 8, n_ext) * at_row[None]
    obs = matmul(same_member, flat(picked).astype(bf16))
    obs3 = obs.reshape(n_mem, 8, n_ext)
    folded = jnp.sum(obs3, axis=0)
    obs_mean = jnp.sum(folded, axis=0, keepdims=True) * (1.0 / big)
    spread = obs - obs_mean
    innovation = observed - obs_mean
    weighted = flat(spread.reshape(n_mem, 8, n_ext) * weight[None])
    gram = jnp.where(same_block, hp(weighted, spread, ((1,), (1,))), 0.0)
    forcing = jnp.sum(weighted * innovation, axis=1, keepdims=True)

    fields3 = jnp.concatenate([states[:, :, W : 2 * W], states[:, :, 3 * W : 4 * W]], axis=2)
    total = jnp.sum(fields3, axis=0)
    centre = (total + pltpu.roll(total, rows, 0)) * (1.0 / ens)
    anomalies = flat(fields3 - centre[None])
    extra = jnp.concatenate([anomalies, jnp.broadcast_to(forcing, (big, W))], axis=1)

    row_sums = jnp.broadcast_to(jnp.sum(jnp.abs(gram), axis=1, keepdims=True), (big, W))
    top = jnp.max(row_sums.reshape(n_mem, 8, W), axis=0)
    top = jnp.maximum(top, pltpu.roll(top, rows, 0))
    bound = (ens - 1.0) + jnp.broadcast_to(top[None], (n_mem, 8, W)).reshape(big, W)[:, 0:1]
    upper = ((ens - 1.0) * identity + gram) / bound
    factor = 1.5 * identity - 0.5 * upper
    lower = factor
    upper = hp(upper, factor)
    for step in range(1, NS_ITERS):
        factor = 1.5 * identity - 0.5 * hp(lower, upper)
        if step < NS_ITERS - 1:
            upper = hp(upper, factor)
            lower = hp(factor, lower)
    rooted = hp(factor, hp(lower, extra)) / jnp.sqrt(bound)
    turned, half_shift = rooted[:, 0 : 2 * W], rooted[:, 2 * W : 2 * W + 1]
    shift = jnp.sum((turned * half_shift).reshape(n_mem, 8, 2 * W), axis=0)
    base = centre + shift + pltpu.roll(shift, rows, 0)
    updated = (math.sqrt(ens - 1.0) * turned).reshape(n_mem, 8, 2 * W) + base[None]
    for j in range(members):
        for var in range(2):
            moved[:, j, var] = updated[:, j * rows : (j + 1) * rows, var * W : (var + 1) * W].astype(bf16)

    def here(k):
        return out_ref.at[:, :, :, pl.ds(pl.multiple_of(k * W, W), W)]

    def back_copy(mem):
        return pltpu.make_async_remote_copy(
            src_ref=moved.at[mem], dst_ref=here(u),
            send_sem=back_send.at[mem], recv_sem=back_recv.at[u],
            device_id={"mem": mem, "lat": t}, device_id_type=MESH,
        )

    own_back = pltpu.make_async_copy(moved.at[u], here(u), back_recv.at[u])

    def send_back(k, carry):
        back_copy(partner(k)).start()
        return carry

    lax.fori_loop(0, n_mem - 1, send_back, 0)
    own_back.start()

    def drain(k, carry):
        mem = partner(k)
        tile_copy(mem).wait_send()
        beside_both(mem, "wait_send")
        return carry

    lax.fori_loop(0, n_mem - 1, drain, 0)
    beside_both(u, "wait_send")
    pl.when(above)(lambda: each(up_halo, "wait_send"))
    pl.when(below)(lambda: each(down_halo, "wait_send"))
    for slot in range(4):
        pl.when(meta_to[slot])(metas[slot].wait_send)
    own_back.wait()

    def wait_back(k, carry):
        mem = partner(k)
        back_copy(mem).wait_send()
        pltpu.make_async_copy(moved.at[mem], here(mem), back_recv.at[mem]).wait()
        return carry

    lax.fori_loop(0, n_mem - 1, wait_back, 0)


def tree(terms):
    while len(terms) > 1:
        terms = [terms[i] + terms[i + 1] for i in range(0, len(terms), 2)]
    return terms[0]


def columns_of(pair, picks):
    return [[jnp.take_along_axis(x, pick, axis=1, mode="promise_in_bounds") for pick in picks] for x in pair]


def product(columns, pair):
    spread_rows = [jnp.broadcast_to(pair[k // 8][k % 8 : k % 8 + 1], (8, W)) for k in range(16)]
    return [tree([a * b for a, b in zip(half, spread_rows)]) for half in columns]


def kernel_compact(
    n_mem, n_lat,
    prior_hbm, wind_hbm, cell_hbm, value_hbm, prec_hbm, nb_hbm, cnt_hbm,
    out_ref,
    prior, wind, cells, value, prec, nb, cnt, meta, packed, tiles, beside, moved, laid,
    load_sem, halo_send, halo_recv, meta_send, meta_recv, tile_send, tile_recv, back_send, back_recv, ready,
):
    f32, bf16, i32 = jnp.float32, jnp.bfloat16, jnp.int32
    u = lax.axis_index("mem")
    t = lax.axis_index("lat")
    members, _, rows, cols = prior_hbm.shape
    slots = nb_hbm.shape[2]
    n_obs = cell_hbm.shape[1]
    ens = members * n_mem
    big = ens * rows
    half = members * rows

    lat_up, lat_down, mem_up, mem_down = t + 1, t - 1, u + 1, u - 1
    above, below = t < n_lat - 1, t > 0
    east_of, west_of = u < n_mem - 1, u > 0
    lats = 1 + above.astype(i32) + below.astype(i32)

    def partner(k):
        up = k + (k >= u).astype(i32)
        k = n_mem - 1 - k
        return jnp.where(2 * u >= n_mem, up, k - (k <= u).astype(i32))

    def signal(sem, mem, lat):
        pl.semaphore_signal(sem, inc=1, device_id={"mem": mem, "lat": lat}, device_id_type=MESH)

    loads = [
        pltpu.make_async_copy(src, dst, load_sem.at[i])
        for i, (src, dst) in enumerate((
            (prior_hbm, prior.at[1]), (wind_hbm, wind.at[1]), (cell_hbm, cells), (value_hbm, value),
            (prec_hbm, prec), (nb_hbm, nb), (cnt_hbm, cnt),
        ))
    ]
    for load in loads:
        load.start()

    barrier = pltpu.get_barrier_semaphore()
    pl.when(above)(lambda: signal(barrier, u, lat_up))
    pl.when(below)(lambda: signal(barrier, u, lat_down))

    def greet(d, carry):
        mem = n_mem - 1 - d
        signal(barrier, mem, t)
        pl.when(above)(lambda: signal(barrier, mem, lat_up))
        pl.when(below)(lambda: signal(barrier, mem, lat_down))
        return carry

    lax.fori_loop(0, n_mem - 1 - u, greet, 0)
    pl.semaphore_wait(barrier, lats * (u + 1) - 1)
    def answer(mem, carry):
        pl.when(below)(lambda: signal(ready.at[2], mem, lat_down))
        signal(ready.at[0], mem, t)
        pl.when(above)(lambda: signal(ready.at[1], mem, lat_up))
        return carry

    lax.fori_loop(0, u, answer, 0)
    for load in loads[:2]:
        load.wait()

    def halo_copies(step):
        return [
            pltpu.make_async_remote_copy(
                src_ref=ref.at[1], dst_ref=ref.at[1 - step],
                send_sem=halo_send.at[1 - step, kind], recv_sem=halo_recv.at[1 - step, kind],
                device_id={"mem": u, "lat": t + step}, device_id_type=MESH,
            )
            for kind, ref in enumerate((prior, wind))
        ]

    def each(copies, act):
        for copy in copies:
            getattr(copy, act)()

    odd = lax.rem(t, 2) == 1
    halo_steps = ((1, above, below), (-1, below, above))
    pl.when(odd & above)(lambda: each(halo_copies(1), "start"))
    pl.when(below)(lambda: each(halo_copies(-1), "start"))
    pl.when(jnp.logical_not(odd) & above)(lambda: each(halo_copies(1), "start"))

    for load in loads[2:]:
        load.wait()
    meta[0, 0:1, :] = cells[...].astype(f32)
    meta[0, 1:2, :] = value[...]
    meta[0, 2:3, :] = prec[...]
    meta[0, 3:8, :] = jnp.zeros((5, n_obs), f32)
    metas = [
        pltpu.make_async_remote_copy(
            src_ref=meta.at[0], dst_ref=meta.at[slot + 1],
            send_sem=meta_send.at[slot], recv_sem=meta_recv.at[slot],
            device_id={"mem": mem, "lat": lat}, device_id_type=MESH,
        )
        for slot, (mem, lat) in enumerate(((u, lat_up), (u, lat_down), (mem_up, t), (mem_down, t)))
    ]
    meta_to = (above, below, east_of, west_of)
    meta_from = (below, above, west_of, east_of)

    def meta_zero(slot):
        meta[slot + 1] = jnp.zeros((8, n_obs), f32)

    for slot in (0, 1, 3):
        pl.when(meta_to[slot])(metas[slot].start)
    for slot in range(4):
        pl.when(jnp.logical_not(meta_from[slot]))(functools.partial(meta_zero, slot))

    n_ext = 5 * n_obs
    n_hi = n_ext // W
    listed = jnp.concatenate([nb[r] for r in range(rows)], axis=1)
    counts = jnp.concatenate(
        [jnp.broadcast_to(cnt[:, r : r + 1], (1, slots)) for r in range(rows)], axis=1
    )
    position = lax.broadcasted_iota(i32, (1, rows * slots), 1)
    hi = lax.shift_right_logical(listed, 7)
    lo = lax.bitwise_and(listed, W - 1)
    hi = jnp.where(lax.bitwise_and(position, slots - 1) < counts, hi, n_hi + 8)
    sub = lax.broadcasted_iota(i32, (8 * n_hi, rows * slots), 0)
    owner = position // slots
    key = hi * 8 + owner
    left = (sub == key).astype(f32) + (sub == key + rows).astype(f32)
    right = (lax.broadcasted_iota(i32, (W, rows * slots), 0) == lo).astype(f32)
    member = matmul(left.astype(bf16), right.astype(bf16), ((1,), (1,)))
    member = jnp.concatenate([member[8 * h : 8 * h + 8] for h in range(n_hi)], axis=1)

    for step, _, came in halo_steps:
        pl.when(came)(lambda: each(halo_copies(step), "wait_recv"))
    col_id = lax.broadcasted_iota(i32, (8, cols), 1)
    row_in = lax.bitwise_and(lax.broadcasted_iota(i32, (8, cols), 0), rows - 1)
    at_bottom, at_top = row_in == 0, row_in == rows - 1
    not_west, not_east = col_id > 0, col_id < cols - 1
    band_ok = [below, None, above]

    def masked(b, x):
        return x if band_ok[b] is None else jnp.where(band_ok[b], x, 0.0)

    flows = []
    for b in range(3):
        east, north = (jnp.concatenate([wind[b, way], wind[b, way]], axis=0) for way in range(2))
        flows.append((
            jnp.maximum(east, 0.0), jnp.minimum(east, 0.0), jnp.maximum(north, 0.0), jnp.minimum(north, 0.0),
        ))
    ahead = []
    for var in range(2):
        kappa = KAPPA[var]
        bands = range(3)
        first_band, last_band = bands[0], bands[-1]
        coef, q = {}, {}
        for b in bands:
            east_pos, east_neg, north_pos, north_neg = flows[b]
            coef[b] = (
                masked(b, 1.0 - (east_pos - east_neg + north_pos - north_neg) - 4.0 * kappa),
                masked(b, jnp.where(not_west, east_pos + kappa, 0.0)),
                masked(b, jnp.where(not_east, kappa - east_neg, 0.0)),
                masked(b, north_pos + kappa),
                masked(b, kappa - north_neg),
            )
            q[b] = masked(b, jnp.concatenate([prior[b, j, var].astype(f32) for j in range(members)], axis=0))
        for s in range(1, SECTIONS + 1):
            new = {}
            for b in bands if s < SECTIONS else bands[1:-1]:
                keep, from_west, from_east, from_south, from_north = coef[b]
                south, north = pltpu.roll(q[b], 1, 0), pltpu.roll(q[b], 7, 0)
                if b > first_band:
                    south = jnp.where(at_bottom, pltpu.roll(q[b - 1], 5, 0), south)
                if b < last_band:
                    north = jnp.where(at_top, pltpu.roll(q[b + 1], 3, 0), north)
                new[b] = (
                    keep * q[b]
                    + from_west * pltpu.roll(q[b], 1, 1)
                    + from_east * pltpu.roll(q[b], cols - 1, 1)
                    + from_south * south
                    + from_north * north
                )
            q = new
        ahead.append({b: x.astype(bf16) for b, x in q.items()})
    for k in range(n_mem):
        for place, (var, b, tile) in enumerate((
            (0, 1, (k - 1) % n_mem), (0, 1, k), (0, 1, (k + 1) % n_mem), (1, 1, k),
        )):
            packed[k, :, place * W : (place + 1) * W] = ahead[var][b][:, tile * W : (tile + 1) * W]

    def tile_copy(mem):
        return pltpu.make_async_remote_copy(
            src_ref=packed.at[mem], dst_ref=tiles.at[u],
            send_sem=tile_send.at[0, mem], recv_sem=tile_recv.at[0, u],
            device_id={"mem": mem, "lat": t}, device_id_type=MESH,
        )

    def beside_copy(mem, side):
        return pltpu.make_async_remote_copy(
            src_ref=packed.at[mem, :, pl.ds(W, W)], dst_ref=beside.at[side, u],
            send_sem=tile_send.at[1 + side, mem], recv_sem=tile_recv.at[1 + side, u],
            device_id={"mem": mem, "lat": t + 1 - 2 * side}, device_id_type=MESH,
        )

    def known(at):
        pl.when(east_of)(lambda: pl.semaphore_wait(ready.at[at], n_mem - 1 - u))

    def send_beside(side):
        known(2 - side)

        def one(k, carry):
            beside_copy(partner(k), side).start()
            return carry

        lax.fori_loop(0, n_mem - 1, one, 0)
        beside_copy(u, side).start()

    def send_tiles(k, carry):
        tile_copy(partner(k)).start()
        return carry

    pl.when(below)(lambda: send_beside(1))
    known(0)
    lax.fori_loop(0, n_mem - 1, send_tiles, 0)
    pl.when(above)(lambda: send_beside(0))
    pl.when(east_of)(metas[2].start)
    own_tile = pltpu.make_async_copy(packed.at[u], tiles.at[u], tile_recv.at[0, u])
    own_tile.start()

    def beside_zero(side):
        beside[side] = jnp.zeros(beside.shape[1:], bf16)

    pl.when(jnp.logical_not(below))(lambda: beside_zero(0))
    pl.when(jnp.logical_not(above))(lambda: beside_zero(1))

    for slot in range(4):
        pl.when(meta_from[slot])(metas[slot].wait_recv)
    cell = jnp.concatenate([meta[i, 0:1, :] for i in range(5)], axis=1)
    observed = jnp.concatenate([meta[i, 1:2, :] for i in range(5)], axis=1)
    valid = (None,) + meta_from
    precision = jnp.concatenate(
        [meta[0, 2:3, :]] + [jnp.where(valid[i], meta[i, 2:3, :], 0.0) for i in range(1, 5)], axis=1
    )
    cell_row = jnp.floor(cell * (1.0 / W))
    cell_col = cell - W * cell_row

    def spread_out(shifts):
        return jnp.concatenate([jnp.full((1, n_obs), s, f32) for s in shifts], axis=1)

    ext_row = cell_row + spread_out((0.0, -float(rows), float(rows), 0.0, 0.0))
    ext_col = cell_col + spread_out((0.0, 0.0, 0.0, -float(W), float(W)))
    block = lax.bitwise_and(lax.broadcasted_iota(i32, (8, n_ext), 0), rows - 1).astype(f32)
    row_gap = (ext_row - block) * (1.0 / LOC_ROWS)
    col_gap = (ext_col - 0.5 * (W - 1)) * (1.0 / LOC_COLS)
    weight = member * jnp.exp(-0.5 * (row_gap * row_gap + col_gap * col_gap)) * precision
    select = (lax.broadcasted_iota(i32, (W, n_ext), 0).astype(f32) == cell_col).astype(f32).astype(bf16)
    lane, sub = lax.broadcasted_iota(i32, (8, W), 1), lax.broadcasted_iota(i32, (8, W), 0)
    lane_block = lax.bitwise_and(lane // ens, rows - 1)
    picks = [lane - lax.bitwise_and(lane, ens - 1) + k for k in range(ens)]
    unit = [(lax.bitwise_and(lane, ens - 1) == sub + 8 * h).astype(f32) for h in range(2)]
    in_block = [lane_block == r for r in range(rows)]
    of_row = [lax.bitwise_and(sub, rows - 1) == r for r in range(rows)]
    mine = lane_block == lax.bitwise_and(sub, rows - 1)
    in_row = [cell_row == float(r) for r in range(rows - 1)]
    own_tile.wait()

    def wait_tiles(k, carry):
        mem = partner(k)
        pltpu.make_async_copy(packed.at[0], tiles.at[mem], tile_recv.at[0, mem]).wait()
        return carry

    def wait_beside(side):
        def wait_one(mem, carry):
            pltpu.make_async_copy(
                packed.at[0, :, pl.ds(W, W)], beside.at[side, mem], tile_recv.at[1 + side, mem]
            ).wait()
            return carry

        lax.fori_loop(0, n_mem, wait_one, 0)

    lax.fori_loop(0, n_mem - 1, wait_tiles, 0)
    pl.when(below)(lambda: wait_beside(0))
    pl.when(above)(lambda: wait_beside(1))

    def flat(x):
        return x.reshape(big, x.shape[-1])

    for at in range(4):
        laid[at] = flat(tiles[:, :, at * W : (at + 1) * W]).astype(f32)
    for side in range(2):
        laid[4 + side] = flat(beside[side]).astype(f32)
    by_row = [[laid[at, pl.ds(r, ens, stride=rows), :] for at in range(6)] for r in range(rows)]
    obs = []
    for i, at in enumerate((1, 4, 5, 0, 2)):
        x = jnp.concatenate([q[at] for q in by_row], axis=0)
        here_obs = slice(i * n_obs, (i + 1) * n_obs)
        x = matmul(x.astype(bf16), select[:, here_obs])
        best = x[(rows - 1) * ens : rows * ens]
        for r in range(rows - 1):
            best = jnp.where(in_row[r][:, here_obs], x[r * ens : (r + 1) * ens], best)
        obs.append(best)
    obs = jnp.concatenate(obs, axis=1)
    obs_mean = jnp.sum(obs[0:8] + obs[8:16], axis=0, keepdims=True) * (1.0 / ens)
    spread = obs - obs_mean
    innovation = jnp.broadcast_to(observed - obs_mean, (8, n_ext))
    w_high, w_low = halves(jnp.concatenate([spread * weight[r : r + 1] for r in range(rows)], axis=0))
    s_high, s_low = halves(jnp.concatenate([spread] * 8 + [innovation], axis=0))
    across = ((1,), (1,))
    two = matmul(jnp.concatenate([w_high, w_low], axis=0), s_high, across)
    sums = two[0:big] + (two[big : 2 * big] + matmul(w_high, s_low, across))
    forcing = jnp.broadcast_to(sums[:, W : W + 1], (big, W))
    gram = []
    for h in range(2):
        part = sums[8 * h : 8 * h + 8, 0:W]
        for r in range(1, rows):
            part = jnp.where(in_block[r], sums[r * ens + 8 * h : r * ens + 8 * h + 8, 0:W], part)
        gram.append(part)

    anomalies, centre = [], jnp.zeros((8, 2 * W), f32)
    for r in range(rows):
        x = jnp.concatenate([by_row[r][1], by_row[r][3]], axis=1)
        mean = jnp.sum(x[0:8] + x[8:16], axis=0, keepdims=True) * (1.0 / ens)
        anomalies.append(x - mean)
        centre = jnp.where(jnp.concatenate([of_row[r]] * 2, axis=1), jnp.broadcast_to(mean, (8, 2 * W)), centre)
    e_high, e_low = halves(jnp.concatenate([jnp.concatenate(anomalies, axis=0), forcing], axis=1))
    extra = jnp.concatenate([e_high, e_low], axis=0)

    def combined(p, x, q, y):
        return [p * a + q * b for a, b in zip(x, y)]

    columns = columns_of(gram, picks)
    row_sums = [tree([jnp.abs(c) for c in half]) for half in columns]
    top = jnp.max(jnp.maximum(row_sums[0], row_sums[1]), axis=0, keepdims=True)
    bound = (ens - 1.0) + jnp.broadcast_to(top, (8, W))
    scale = 1.0 / bound
    end_scale = 1.0 / jnp.sqrt(bound)

    def system_times(x):
        return [scale * y for y in combined(ens - 1.0, x, 1.0, product(columns, x))]

    joint = [scale * y for y in combined(ens - 1.0, unit, 1.0, gram)]
    lower = combined(1.5, unit, -0.5, joint)
    half_way = combined(1.5, joint, -0.5, system_times(joint))
    joint = combined(1.5, half_way, -0.5, system_times(half_way))
    for step in range(1, NS_ITERS - 1):
        columns = columns_of(joint, picks)
        half_way = combined(1.5, joint, -0.5, product(columns, joint))
        lower = combined(1.5, lower, -0.5, product(columns, lower))
        joint = combined(1.5, half_way, -0.5, product(columns, half_way))
    root = combined(1.5, lower, -0.5, product(columns_of(lower, picks), joint))
    root = [x * end_scale for x in root]
    root_rows = []
    for v in range(big // 8):
        side, at = root[v // 4], (2 * v) % 8
        pair = jnp.where(
            sub < rows,
            jnp.broadcast_to(side[at : at + 1], (8, W)),
            jnp.broadcast_to(side[at + 1 : at + 2], (8, W)),
        )
        root_rows.append(jnp.where(mine, pair, 0.0))
    r_high, r_low = halves(jnp.concatenate(root_rows, axis=0))
    two = matmul(jnp.concatenate([r_high, r_low], axis=0), extra)
    rooted = two[0:big] + two[big : 2 * big]
    turned, half_shift = rooted[:, 0 : 2 * W], rooted[:, 2 * W : 3 * W]
    half_shift = jnp.concatenate([half_shift, half_shift], axis=1)
    shift = jnp.sum((turned * half_shift).reshape(n_mem, 8, 2 * W), axis=0)
    base = centre + shift + pltpu.roll(shift, rows, 0)
    updated = (math.sqrt(ens - 1.0) * turned).reshape(n_mem, 8, 2 * W) + base[None]
    for j in range(members):
        for var in range(2):
            moved[:, j, var] = updated[:, j * rows : (j + 1) * rows, var * W : (var + 1) * W].astype(bf16)

    def here(k):
        return out_ref.at[:, :, :, pl.ds(pl.multiple_of(k * W, W), W)]

    def back_copy(mem):
        return pltpu.make_async_remote_copy(
            src_ref=moved.at[mem], dst_ref=here(u),
            send_sem=back_send.at[mem], recv_sem=back_recv.at[u],
            device_id={"mem": mem, "lat": t}, device_id_type=MESH,
        )

    own_back = pltpu.make_async_copy(moved.at[u], here(u), back_recv.at[u])

    def send_back(k, carry):
        back_copy(partner(k)).start()
        return carry

    lax.fori_loop(0, n_mem - 1, send_back, 0)
    own_back.start()

    def drain(k, carry):
        mem = partner(k)
        tile_copy(mem).wait_send()
        pl.when(above)(lambda: beside_copy(mem, 0).wait_send())
        pl.when(below)(lambda: beside_copy(mem, 1).wait_send())
        return carry

    lax.fori_loop(0, n_mem - 1, drain, 0)
    pl.when(above)(lambda: beside_copy(u, 0).wait_send())
    pl.when(below)(lambda: beside_copy(u, 1).wait_send())
    for step, to, _ in halo_steps:
        pl.when(to)(lambda: each(halo_copies(step), "wait_send"))
    for slot in range(4):
        pl.when(meta_to[slot])(metas[slot].wait_send)
    own_back.wait()

    def wait_back(k, carry):
        mem = partner(k)
        back_copy(mem).wait_send()
        pltpu.make_async_copy(moved.at[mem], here(mem), back_recv.at[mem]).wait()
        return carry

    lax.fori_loop(0, n_mem - 1, wait_back, 0)


def compact_call(n_mem, n_lat, prior, wind, cell, value, prec, nb, cnt):
    members, _, rows, cols = prior.shape
    n_obs = cell.shape[1]
    f32, bf16 = jnp.float32, jnp.bfloat16
    dma = pltpu.SemaphoreType.DMA
    return pl.pallas_call(
        functools.partial(kernel_compact, n_mem, n_lat),
        out_shape=pltpu.VMEM(prior.shape, bf16),
        in_specs=[pl.BlockSpec(memory_space=pl.ANY)] * 7,
        out_specs=pl.BlockSpec(memory_space=pltpu.VMEM),
        scratch_shapes=[
            pltpu.VMEM((3,) + prior.shape, bf16),
            pltpu.VMEM((3,) + wind.shape, f32),
            pltpu.VMEM(cell.shape, jnp.int32),
            pltpu.VMEM(value.shape, f32),
            pltpu.VMEM(prec.shape, f32),
            pltpu.VMEM(nb.shape, jnp.int32),
            pltpu.VMEM(cnt.shape, jnp.int32),
            pltpu.VMEM((5, 8, n_obs), f32),
            pltpu.VMEM((n_mem, members * rows, 4 * W), bf16),
            pltpu.VMEM((n_mem, members * rows, 4 * W), bf16),
            pltpu.VMEM((2, n_mem, members * rows, W), bf16),
            pltpu.VMEM((n_mem, members, 2, rows, W), bf16),
            pltpu.VMEM((6, n_mem * members * rows, W), f32),
            dma((7,)), dma((3, 2)), dma((3, 2)), dma((4,)), dma((4,)),
            dma((3, n_mem)), dma((3, n_mem)), dma((n_mem,)), dma((n_mem,)), pltpu.SemaphoreType.REGULAR((3,)),
        ],
        compiler_params=pltpu.CompilerParams(collective_id=0, has_side_effects=True),
    )(prior, wind, cell, value, prec, nb, cnt)


def on_device(n_mem, n_lat, *args):
    prior, wind, cell, value, prec, nb, cnt = args
    cnt = cnt.T
    members, _, rows, cols = prior.shape
    if members * n_mem == 16 and members == 2 and rows == 4:
        return compact_call(n_mem, n_lat, prior, wind, cell, value, prec, nb, cnt)
    n_obs = cell.shape[1]
    f32, bf16, i32 = jnp.float32, jnp.bfloat16, jnp.int32
    dma = pltpu.SemaphoreType.DMA
    return pl.pallas_call(
        functools.partial(kernel, n_mem, n_lat),
        out_shape=pltpu.VMEM(prior.shape, bf16),
        in_specs=[pl.BlockSpec(memory_space=pl.ANY)] * 7,
        out_specs=pl.BlockSpec(memory_space=pltpu.VMEM),
        scratch_shapes=[
            pltpu.VMEM((3,) + prior.shape, bf16),
            pltpu.VMEM((3,) + wind.shape, f32),
            pltpu.VMEM(cell.shape, i32),
            pltpu.VMEM(value.shape, f32),
            pltpu.VMEM(prec.shape, f32),
            pltpu.VMEM(nb.shape, i32),
            pltpu.VMEM(cnt.shape, i32),
            pltpu.VMEM((5, 8, n_obs), f32),
            pltpu.VMEM((n_mem, members * rows, 4 * W), bf16),
            pltpu.VMEM((n_mem, members * rows, 4 * W), bf16),
            pltpu.VMEM((2, n_mem, members * rows, W), bf16),
            pltpu.VMEM((n_mem, members, 2, rows, W), bf16),
            dma((7,)), dma((2, 2)), dma((2, 2)), dma((4,)), dma((4,)),
            dma((3, n_mem)), dma((3, n_mem)), dma((n_mem,)), dma((n_mem,)), pltpu.SemaphoreType.REGULAR,
        ],
        compiler_params=pltpu.CompilerParams(collective_id=0, has_side_effects=True),
    )(prior, wind, cell, value, prec, nb, cnt)


def solution(mesh):
    placed = (
        P("mem", None, "lat", None),
        P(None, "lat", None),
        P("lat", "mem"),
        P("lat", "mem"),
        P("lat", "mem"),
        P("lat", "mem", None),
        P("lat", "mem"),
    )
    return jax.shard_map(
        functools.partial(on_device, mesh.shape["mem"], mesh.shape["lat"]),
        mesh=mesh,
        in_specs=placed,
        out_specs=P("mem", None, "lat", None),
        check_vma=False,
    )
```

```python
import functools
import math

import jax
import jax.numpy as jnp
from jax import lax
from jax.experimental import pallas as pl
from jax.experimental.pallas import tpu as pltpu
from jax.sharding import PartitionSpec as P

W = 128
SECTIONS = 4
NS_ITERS = 6
LOC_ROWS = 2
LOC_COLS = 64
KAPPA = (0.025, 0.0125)
MESH = pl.DeviceIdType.MESH


def matmul(a, b, contract=((1,), (0,))):
    return lax.dot_general(a, b, (contract, ((), ())), preferred_element_type=jnp.float32)


def halves(x):
    high = x.astype(jnp.bfloat16)
    return high, (x - high.astype(jnp.float32)).astype(jnp.bfloat16)


def hp(a, b, contract=((1,), (0,))):
    a_high, a_low = halves(a)
    b_high, b_low = halves(b)
    return matmul(a_high, b_high, contract) + (
        matmul(a_high, b_low, contract) + matmul(a_low, b_high, contract)
    )


def kernel(
    n_mem, n_lat,
    prior_hbm, wind_hbm, cell_hbm, value_hbm, prec_hbm, nb_hbm, cnt_hbm,
    out_ref,
    prior, wind, cells, value, prec, nb, cnt, meta, packed, tiles, beside, moved,
    load_sem, halo_send, halo_recv, meta_send, meta_recv, tile_send, tile_recv, back_send, back_recv, ready,
):
    f32, bf16, i32 = jnp.float32, jnp.bfloat16, jnp.int32
    u = lax.axis_index("mem")
    t = lax.axis_index("lat")
    members, _, rows, cols = prior_hbm.shape
    slots = nb_hbm.shape[2]
    n_obs = cell_hbm.shape[1]
    ens = members * n_mem
    big = ens * rows
    half = members * rows

    lat_up, lat_down, mem_up, mem_down = t + 1, t - 1, u + 1, u - 1
    above, below = t < n_lat - 1, t > 0
    east_of, west_of = u < n_mem - 1, u > 0
    lats = 1 + above.astype(i32) + below.astype(i32)

    def partner(k):
        up = k + (k >= u).astype(i32)
        k = n_mem - 1 - k
        return jnp.where(2 * u >= n_mem, up, k - (k <= u).astype(i32))

    def signal(sem, mem, lat):
        pl.semaphore_signal(sem, inc=1, device_id={"mem": mem, "lat": lat}, device_id_type=MESH)

    def signal_lats(sem, mem):
        signal(sem, mem, t)
        pl.when(above)(lambda: signal(sem, mem, lat_up))
        pl.when(below)(lambda: signal(sem, mem, lat_down))

    loads = [
        pltpu.make_async_copy(src, dst, load_sem.at[i])
        for i, (src, dst) in enumerate((
            (prior_hbm, prior.at[1]), (wind_hbm, wind.at[1]), (cell_hbm, cells), (value_hbm, value),
            (prec_hbm, prec), (nb_hbm, nb), (cnt_hbm, cnt),
        ))
    ]
    for load in loads:
        load.start()

    barrier = pltpu.get_barrier_semaphore()
    pl.when(above)(lambda: signal(barrier, u, lat_up))
    pl.when(below)(lambda: signal(barrier, u, lat_down))

    def greet(d, carry):
        signal_lats(barrier, n_mem - 1 - d)
        return carry

    lax.fori_loop(0, n_mem - 1 - u, greet, 0)
    pl.semaphore_wait(barrier, lats * (u + 1) - 1)
    for load in loads[:2]:
        load.wait()

    def halo_copies(side, lat):
        return [
            pltpu.make_async_remote_copy(
                src_ref=src, dst_ref=dst.at[2 * side],
                send_sem=halo_send.at[side, kind], recv_sem=halo_recv.at[side, kind],
                device_id={"mem": u, "lat": lat}, device_id_type=MESH,
            )
            for kind, (src, dst) in enumerate(((prior.at[1], prior), (wind.at[1], wind)))
        ]

    def each(copies, act):
        for copy in copies:
            getattr(copy, act)()

    up_halo, down_halo = halo_copies(0, lat_up), halo_copies(1, lat_down)
    pl.when(above)(lambda: each(up_halo, "start"))
    pl.when(below)(lambda: each(down_halo, "start"))

    def answer(mem, carry):
        signal_lats(ready, mem)
        return carry

    lax.fori_loop(0, u, answer, 0)

    for load in loads[2:]:
        load.wait()
    meta[0, 0:1, :] = cells[...].astype(f32)
    meta[0, 1:2, :] = value[...]
    meta[0, 2:3, :] = prec[...]
    meta[0, 3:8, :] = jnp.zeros((5, n_obs), f32)
    metas = [
        pltpu.make_async_remote_copy(
            src_ref=meta.at[0], dst_ref=meta.at[slot + 1],
            send_sem=meta_send.at[slot], recv_sem=meta_recv.at[slot],
            device_id={"mem": mem, "lat": lat}, device_id_type=MESH,
        )
        for slot, (mem, lat) in enumerate(((u, lat_up), (u, lat_down), (mem_up, t), (mem_down, t)))
    ]
    meta_to = (above, below, east_of, west_of)
    meta_from = (below, above, west_of, east_of)

    def meta_zero(slot):
        meta[slot + 1] = jnp.zeros((8, n_obs), f32)

    for slot in (0, 1, 3):
        pl.when(meta_to[slot])(metas[slot].start)
    for slot in range(4):
        pl.when(jnp.logical_not(meta_from[slot]))(functools.partial(meta_zero, slot))

    n_ext = 5 * n_obs
    n_hi = n_ext // W
    listed = jnp.concatenate([nb[r] for r in range(rows)], axis=1)
    counts = jnp.concatenate(
        [jnp.broadcast_to(cnt[:, r : r + 1], (1, slots)) for r in range(rows)], axis=1
    )
    position = lax.broadcasted_iota(i32, (1, rows * slots), 1)
    hi = lax.shift_right_logical(listed, 7)
    lo = lax.bitwise_and(listed, W - 1)
    hi = jnp.where(lax.bitwise_and(position, slots - 1) < counts, hi, n_hi + 8)
    sub = lax.broadcasted_iota(i32, (8 * n_hi, rows * slots), 0)
    owner = position // slots
    key = hi * 8 + owner
    left = (sub == key).astype(f32) + (sub == key + rows).astype(f32)
    right = (lax.broadcasted_iota(i32, (W, rows * slots), 0) == lo).astype(f32)
    member = matmul(left.astype(bf16), right.astype(bf16), ((1,), (1,)))
    member = jnp.concatenate([member[8 * h : 8 * h + 8] for h in range(n_hi)], axis=1)

    pl.when(below)(lambda: each(up_halo, "wait_recv"))
    pl.when(above)(lambda: each(down_halo, "wait_recv"))
    wide = 4 * rows
    row_id = lax.broadcasted_iota(i32, (wide, cols), 0)
    col_id = lax.broadcasted_iota(i32, (wide, cols), 1)
    first_row = jnp.where(t == 0, rows, 0)
    last_row = jnp.where(t == n_lat - 1, 2 * rows, 3 * rows)
    inside = (row_id >= first_row) & (row_id < last_row)

    def band(parts):
        return jnp.concatenate(list(parts) + [jnp.zeros((rows, cols), f32)], axis=0)

    east = band(wind[s, 0] for s in range(3))
    north = band(wind[s, 1] for s in range(3))
    east_pos, east_neg = jnp.maximum(east, 0.0), jnp.minimum(east, 0.0)
    north_pos, north_neg = jnp.maximum(north, 0.0), jnp.minimum(north, 0.0)
    fields = []
    for var in range(2):
        kappa = KAPPA[var]
        keep = jnp.where(inside, 1.0 - (east_pos - east_neg + north_pos - north_neg) - 4.0 * kappa, 0.0)
        from_west = jnp.where(inside & (col_id > 0), east_pos + kappa, 0.0)
        from_east = jnp.where(inside & (col_id < cols - 1), kappa - east_neg, 0.0)
        from_south = jnp.where(inside, north_pos + kappa, 0.0)
        from_north = jnp.where(inside, kappa - north_neg, 0.0)
        own = []
        for j in range(members):
            q = jnp.where(inside, band(prior[s, j, var].astype(f32) for s in range(3)), 0.0)
            for _ in range(SECTIONS):
                q = (
                    keep * q
                    + from_west * pltpu.roll(q, 1, 1)
                    + from_east * pltpu.roll(q, cols - 1, 1)
                    + from_south * pltpu.roll(q, 1, 0)
                    + from_north * pltpu.roll(q, wide - 1, 0)
                )
            own.append(q[rows : 2 * rows])
        fields.append(jnp.concatenate(own, axis=0).astype(bf16))
    for k in range(n_mem):
        for place, (var, tile) in enumerate(((0, (k - 1) % n_mem), (0, k), (0, (k + 1) % n_mem), (1, k))):
            packed[k, :, place * W : (place + 1) * W] = fields[var][:, tile * W : (tile + 1) * W]

    def beside_copy(mem, side, lat):
        return pltpu.make_async_remote_copy(
            src_ref=packed.at[mem, :, pl.ds(W, W)], dst_ref=beside.at[side, u],
            send_sem=tile_send.at[1 + side, mem], recv_sem=tile_recv.at[1 + side, u],
            device_id={"mem": mem, "lat": lat}, device_id_type=MESH,
        )

    def tile_copy(mem):
        return pltpu.make_async_remote_copy(
            src_ref=packed.at[mem], dst_ref=tiles.at[u],
            send_sem=tile_send.at[0, mem], recv_sem=tile_recv.at[0, u],
            device_id={"mem": mem, "lat": t}, device_id_type=MESH,
        )

    def beside_both(mem, act):
        pl.when(above)(lambda: getattr(beside_copy(mem, 0, lat_up), act)())
        pl.when(below)(lambda: getattr(beside_copy(mem, 1, lat_down), act)())

    pl.when(east_of)(lambda: pl.semaphore_wait(ready, lats * (n_mem - 1 - u)))
    pl.when(east_of)(metas[2].start)

    def send_tiles(k, carry):
        mem = partner(k)
        tile_copy(mem).start()
        beside_both(mem, "start")
        return carry

    lax.fori_loop(0, n_mem - 1, send_tiles, 0)
    beside_both(u, "start")
    own_tile = pltpu.make_async_copy(packed.at[u], tiles.at[u], tile_recv.at[0, u])
    own_tile.start()

    def beside_zero(side):
        beside[side] = jnp.zeros(beside.shape[1:], bf16)

    pl.when(jnp.logical_not(below))(lambda: beside_zero(0))
    pl.when(jnp.logical_not(above))(lambda: beside_zero(1))

    for slot in range(4):
        pl.when(meta_from[slot])(metas[slot].wait_recv)
    cell = jnp.concatenate([meta[i, 0:1, :] for i in range(5)], axis=1)
    observed = jnp.concatenate([meta[i, 1:2, :] for i in range(5)], axis=1)
    valid = (None,) + meta_from
    precision = jnp.concatenate(
        [meta[0, 2:3, :]] + [jnp.where(valid[i], meta[i, 2:3, :], 0.0) for i in range(1, 5)], axis=1
    )
    cell_row = jnp.floor(cell * (1.0 / W))
    cell_col = cell - W * cell_row

    def spread_out(shifts):
        return jnp.concatenate([jnp.full((1, n_obs), s, f32) for s in shifts], axis=1)

    ext_row = cell_row + spread_out((0.0, -float(rows), float(rows), 0.0, 0.0))
    ext_col = cell_col + spread_out((0.0, 0.0, 0.0, -float(W), float(W)))
    block = lax.bitwise_and(lax.broadcasted_iota(i32, (8, n_ext), 0), rows - 1).astype(f32)
    row_gap = (ext_row - block) * (1.0 / LOC_ROWS)
    col_gap = (ext_col - 0.5 * (W - 1)) * (1.0 / LOC_COLS)
    weight = member * jnp.exp(-0.5 * (row_gap * row_gap + col_gap * col_gap)) * precision
    select = (lax.broadcasted_iota(i32, (W, n_ext), 0).astype(f32) == cell_col).astype(f32).astype(bf16)
    at_row = jnp.where(block == cell_row, 1.0, 0.0)
    ids0 = lax.broadcasted_iota(i32, (big, big), 0)
    ids1 = lax.broadcasted_iota(i32, (big, big), 1)
    same_member = (ids0 // rows == ids1 // rows).astype(f32).astype(bf16)
    same_block = lax.bitwise_and(ids0, rows - 1) == lax.bitwise_and(ids1, rows - 1)
    identity = (ids0 == ids1).astype(f32)

    own_tile.wait()

    def wait_tiles(k, carry):
        mem = partner(k)
        pltpu.make_async_copy(packed.at[0], tiles.at[mem], tile_recv.at[0, mem]).wait()
        return carry

    def wait_beside(side):
        def wait_one(mem, carry):
            pltpu.make_async_copy(
                packed.at[0, :, pl.ds(W, W)], beside.at[side, mem], tile_recv.at[1 + side, mem]
            ).wait()
            return carry

        lax.fori_loop(0, n_mem, wait_one, 0)

    lax.fori_loop(0, n_mem - 1, wait_tiles, 0)
    pl.when(below)(lambda: wait_beside(0))
    pl.when(above)(lambda: wait_beside(1))

    states = tiles[...].astype(f32)

    def flat(x):
        return x.reshape(big, x.shape[-1])

    sources = (
        states[:, :, W : 2 * W], beside[0].astype(f32), beside[1].astype(f32),
        states[:, :, 0:W], states[:, :, 2 * W : 3 * W],
    )
    picked = jnp.concatenate(
        [
            matmul(flat(x).astype(bf16), select[:, i * n_obs : (i + 1) * n_obs])
            for i, x in enumerate(sources)
        ],
        axis=1,
    )
    picked = picked.reshape(n_mem, 8, n_ext) * at_row[None]
    obs = matmul(same_member, flat(picked).astype(bf16))
    obs3 = obs.reshape(n_mem, 8, n_ext)
    folded = jnp.sum(obs3, axis=0)
    obs_mean = jnp.sum(folded, axis=0, keepdims=True) * (1.0 / big)
    spread = obs - obs_mean
    innovation = observed - obs_mean
    weighted = flat(spread.reshape(n_mem, 8, n_ext) * weight[None])
    gram = jnp.where(same_block, hp(weighted, spread, ((1,), (1,))), 0.0)
    forcing = jnp.sum(weighted * innovation, axis=1, keepdims=True)

    fields3 = jnp.concatenate([states[:, :, W : 2 * W], states[:, :, 3 * W : 4 * W]], axis=2)
    total = jnp.sum(fields3, axis=0)
    centre = (total + pltpu.roll(total, rows, 0)) * (1.0 / ens)
    anomalies = flat(fields3 - centre[None])
    extra = jnp.concatenate([anomalies, jnp.broadcast_to(forcing, (big, W))], axis=1)

    row_sums = jnp.broadcast_to(jnp.sum(jnp.abs(gram), axis=1, keepdims=True), (big, W))
    top = jnp.max(row_sums.reshape(n_mem, 8, W), axis=0)
    top = jnp.maximum(top, pltpu.roll(top, rows, 0))
    bound = (ens - 1.0) + jnp.broadcast_to(top[None], (n_mem, 8, W)).reshape(big, W)[:, 0:1]
    upper = ((ens - 1.0) * identity + gram) / bound
    factor = 1.5 * identity - 0.5 * upper
    lower = factor
    upper = hp(upper, factor)
    for step in range(1, NS_ITERS):
        factor = 1.5 * identity - 0.5 * hp(lower, upper)
        if step < NS_ITERS - 1:
            upper = hp(upper, factor)
            lower = hp(factor, lower)
    rooted = hp(factor, hp(lower, extra)) / jnp.sqrt(bound)
    turned, half_shift = rooted[:, 0 : 2 * W], rooted[:, 2 * W : 2 * W + 1]
    shift = jnp.sum((turned * half_shift).reshape(n_mem, 8, 2 * W), axis=0)
    base = centre + shift + pltpu.roll(shift, rows, 0)
    updated = (math.sqrt(ens - 1.0) * turned).reshape(n_mem, 8, 2 * W) + base[None]
    for j in range(members):
        for var in range(2):
            moved[:, j, var] = updated[:, j * rows : (j + 1) * rows, var * W : (var + 1) * W].astype(bf16)

    def here(k):
        return out_ref.at[:, :, :, pl.ds(pl.multiple_of(k * W, W), W)]

    def back_copy(mem):
        return pltpu.make_async_remote_copy(
            src_ref=moved.at[mem], dst_ref=here(u),
            send_sem=back_send.at[mem], recv_sem=back_recv.at[u],
            device_id={"mem": mem, "lat": t}, device_id_type=MESH,
        )

    own_back = pltpu.make_async_copy(moved.at[u], here(u), back_recv.at[u])

    def send_back(k, carry):
        back_copy(partner(k)).start()
        return carry

    lax.fori_loop(0, n_mem - 1, send_back, 0)
    own_back.start()

    def drain(k, carry):
        mem = partner(k)
        tile_copy(mem).wait_send()
        beside_both(mem, "wait_send")
        return carry

    lax.fori_loop(0, n_mem - 1, drain, 0)
    beside_both(u, "wait_send")
    pl.when(above)(lambda: each(up_halo, "wait_send"))
    pl.when(below)(lambda: each(down_halo, "wait_send"))
    for slot in range(4):
        pl.when(meta_to[slot])(metas[slot].wait_send)
    own_back.wait()

    def wait_back(k, carry):
        mem = partner(k)
        back_copy(mem).wait_send()
        pltpu.make_async_copy(moved.at[mem], here(mem), back_recv.at[mem]).wait()
        return carry

    lax.fori_loop(0, n_mem - 1, wait_back, 0)


def tree(terms):
    while len(terms) > 1:
        terms = [terms[i] + terms[i + 1] for i in range(0, len(terms), 2)]
    return terms[0]


def columns_of(pair, picks):
    return [[jnp.take_along_axis(x, pick, axis=1, mode="promise_in_bounds") for pick in picks] for x in pair]


def product(columns, pair):
    spread_rows = [jnp.broadcast_to(pair[k // 8][k % 8 : k % 8 + 1], (8, W)) for k in range(16)]
    return [tree([a * b for a, b in zip(half, spread_rows)]) for half in columns]


def kernel_compact(
    n_mem, n_lat,
    prior_hbm, wind_hbm, cell_hbm, value_hbm, prec_hbm, nb_hbm, cnt_hbm,
    out_ref,
    prior, wind, cells, value, prec, nb, cnt, meta, packed, tiles, beside, moved, laid,
    load_sem, halo_send, halo_recv, meta_send, meta_recv, tile_send, tile_recv, back_send, back_recv, ready,
):
    f32, bf16, i32 = jnp.float32, jnp.bfloat16, jnp.int32
    u = lax.axis_index("mem")
    t = lax.axis_index("lat")
    members, _, rows, cols = prior_hbm.shape
    slots = nb_hbm.shape[2]
    n_obs = cell_hbm.shape[1]
    ens = members * n_mem
    big = ens * rows
    half = members * rows

    lat_up, lat_down, mem_up, mem_down = t + 1, t - 1, u + 1, u - 1
    above, below = t < n_lat - 1, t > 0
    east_of, west_of = u < n_mem - 1, u > 0
    lats = 1 + above.astype(i32) + below.astype(i32)

    def partner(k):
        up = k + (k >= u).astype(i32)
        k = n_mem - 1 - k
        return jnp.where(2 * u >= n_mem, up, k - (k <= u).astype(i32))

    def signal(sem, mem, lat):
        pl.semaphore_signal(sem, inc=1, device_id={"mem": mem, "lat": lat}, device_id_type=MESH)

    loads = [
        pltpu.make_async_copy(src, dst, load_sem.at[i])
        for i, (src, dst) in enumerate((
            (prior_hbm, prior.at[1]), (wind_hbm, wind.at[1]), (cell_hbm, cells), (value_hbm, value),
            (prec_hbm, prec), (nb_hbm, nb), (cnt_hbm, cnt),
        ))
    ]
    for load in loads:
        load.start()

    barrier = pltpu.get_barrier_semaphore()
    pl.when(above)(lambda: signal(barrier, u, lat_up))
    pl.when(below)(lambda: signal(barrier, u, lat_down))

    def greet(d, carry):
        mem = n_mem - 1 - d
        signal(barrier, mem, t)
        pl.when(above)(lambda: signal(barrier, mem, lat_up))
        pl.when(below)(lambda: signal(barrier, mem, lat_down))
        return carry

    lax.fori_loop(0, n_mem - 1 - u, greet, 0)
    pl.semaphore_wait(barrier, lats * (u + 1) - 1)
    def answer(mem, carry):
        pl.when(below)(lambda: signal(ready.at[2], mem, lat_down))
        signal(ready.at[0], mem, t)
        pl.when(above)(lambda: signal(ready.at[1], mem, lat_up))
        return carry

    lax.fori_loop(0, u, answer, 0)
    for load in loads[:2]:
        load.wait()

    def halo_copies(step):
        return [
            pltpu.make_async_remote_copy(
                src_ref=ref.at[1], dst_ref=ref.at[1 - step],
                send_sem=halo_send.at[1 - step, kind], recv_sem=halo_recv.at[1 - step, kind],
                device_id={"mem": u, "lat": t + step}, device_id_type=MESH,
            )
            for kind, ref in enumerate((prior, wind))
        ]

    def each(copies, act):
        for copy in copies:
            getattr(copy, act)()

    odd = lax.rem(t, 2) == 1
    halo_steps = ((1, above, below), (-1, below, above))
    pl.when(odd & above)(lambda: each(halo_copies(1), "start"))
    pl.when(below)(lambda: each(halo_copies(-1), "start"))
    pl.when(jnp.logical_not(odd) & above)(lambda: each(halo_copies(1), "start"))

    for load in loads[2:]:
        load.wait()
    meta[0, 0:1, :] = cells[...].astype(f32)
    meta[0, 1:2, :] = value[...]
    meta[0, 2:3, :] = prec[...]
    meta[0, 3:8, :] = jnp.zeros((5, n_obs), f32)
    metas = [
        pltpu.make_async_remote_copy(
            src_ref=meta.at[0], dst_ref=meta.at[slot + 1],
            send_sem=meta_send.at[slot], recv_sem=meta_recv.at[slot],
            device_id={"mem": mem, "lat": lat}, device_id_type=MESH,
        )
        for slot, (mem, lat) in enumerate(((u, lat_up), (u, lat_down), (mem_up, t), (mem_down, t)))
    ]
    meta_to = (above, below, east_of, west_of)
    meta_from = (below, above, west_of, east_of)

    def meta_zero(slot):
        meta[slot + 1] = jnp.zeros((8, n_obs), f32)

    for slot in (0, 1, 3):
        pl.when(meta_to[slot])(metas[slot].start)
    for slot in range(4):
        pl.when(jnp.logical_not(meta_from[slot]))(functools.partial(meta_zero, slot))

    n_ext = 5 * n_obs
    n_hi = n_ext // W
    listed = jnp.concatenate([nb[r] for r in range(rows)], axis=1)
    counts = jnp.concatenate(
        [jnp.broadcast_to(cnt[:, r : r + 1], (1, slots)) for r in range(rows)], axis=1
    )
    position = lax.broadcasted_iota(i32, (1, rows * slots), 1)
    hi = lax.shift_right_logical(listed, 7)
    lo = lax.bitwise_and(listed, W - 1)
    hi = jnp.where(lax.bitwise_and(position, slots - 1) < counts, hi, n_hi + 8)
    sub = lax.broadcasted_iota(i32, (8 * n_hi, rows * slots), 0)
    owner = position // slots
    key = hi * 8 + owner
    left = (sub == key).astype(f32) + (sub == key + rows).astype(f32)
    right = (lax.broadcasted_iota(i32, (W, rows * slots), 0) == lo).astype(f32)
    member = matmul(left.astype(bf16), right.astype(bf16), ((1,), (1,)))
    member = jnp.concatenate([member[8 * h : 8 * h + 8] for h in range(n_hi)], axis=1)

    for step, _, came in halo_steps:
        pl.when(came)(lambda: each(halo_copies(step), "wait_recv"))
    col_id = lax.broadcasted_iota(i32, (8, cols), 1)
    row_in = lax.bitwise_and(lax.broadcasted_iota(i32, (8, cols), 0), rows - 1)
    at_bottom, at_top = row_in == 0, row_in == rows - 1
    not_west, not_east = col_id > 0, col_id < cols - 1
    band_ok = [below, None, above]

    def masked(b, x):
        return x if band_ok[b] is None else jnp.where(band_ok[b], x, 0.0)

    flows = []
    for b in range(3):
        east, north = (jnp.concatenate([wind[b, way], wind[b, way]], axis=0) for way in range(2))
        flows.append((
            jnp.maximum(east, 0.0), jnp.minimum(east, 0.0), jnp.maximum(north, 0.0), jnp.minimum(north, 0.0),
        ))
    ahead = []
    for var in range(2):
        kappa = KAPPA[var]
        bands = range(3)
        first_band, last_band = bands[0], bands[-1]
        coef, q = {}, {}
        for b in bands:
            east_pos, east_neg, north_pos, north_neg = flows[b]
            coef[b] = (
                masked(b, 1.0 - (east_pos - east_neg + north_pos - north_neg) - 4.0 * kappa),
                masked(b, jnp.where(not_west, east_pos + kappa, 0.0)),
                masked(b, jnp.where(not_east, kappa - east_neg, 0.0)),
                masked(b, north_pos + kappa),
                masked(b, kappa - north_neg),
            )
            q[b] = masked(b, jnp.concatenate([prior[b, j, var].astype(f32) for j in range(members)], axis=0))
        for s in range(1, SECTIONS + 1):
            new = {}
            for b in bands if s < SECTIONS else bands[1:-1]:
                keep, from_west, from_east, from_south, from_north = coef[b]
                south, north = pltpu.roll(q[b], 1, 0), pltpu.roll(q[b], 7, 0)
                if b > first_band:
                    south = jnp.where(at_bottom, pltpu.roll(q[b - 1], 5, 0), south)
                if b < last_band:
                    north = jnp.where(at_top, pltpu.roll(q[b + 1], 3, 0), north)
                new[b] = (
                    keep * q[b]
                    + from_west * pltpu.roll(q[b], 1, 1)
                    + from_east * pltpu.roll(q[b], cols - 1, 1)
                    + from_south * south
                    + from_north * north
                )
            q = new
        ahead.append({b: x.astype(bf16) for b, x in q.items()})
    for k in range(n_mem):
        for place, (var, b, tile) in enumerate((
            (0, 1, (k - 1) % n_mem), (0, 1, k), (0, 1, (k + 1) % n_mem), (1, 1, k),
        )):
            packed[k, :, place * W : (place + 1) * W] = ahead[var][b][:, tile * W : (tile + 1) * W]

    def tile_copy(mem):
        return pltpu.make_async_remote_copy(
            src_ref=packed.at[mem], dst_ref=tiles.at[u],
            send_sem=tile_send.at[0], recv_sem=tile_recv.at[0],
            device_id={"mem": mem, "lat": t}, device_id_type=MESH,
        )

    def beside_copy(mem, side):
        return pltpu.make_async_remote_copy(
            src_ref=packed.at[mem, :, pl.ds(W, W)], dst_ref=beside.at[side, u],
            send_sem=tile_send.at[1 + side], recv_sem=tile_recv.at[1 + side],
            device_id={"mem": mem, "lat": t + 1 - 2 * side}, device_id_type=MESH,
        )

    def known(at):
        pl.when(east_of)(lambda: pl.semaphore_wait(ready.at[at], n_mem - 1 - u))

    def send_beside(side):
        known(2 - side)

        def one(k, carry):
            beside_copy(partner(k), side).start()
            return carry

        lax.fori_loop(0, n_mem - 1, one, 0)
        beside_copy(u, side).start()

    def send_tiles(k, carry):
        tile_copy(partner(k)).start()
        return carry

    pl.when(below)(lambda: send_beside(1))
    known(0)
    lax.fori_loop(0, n_mem - 1, send_tiles, 0)
    pl.when(above)(lambda: send_beside(0))
    pl.when(east_of)(metas[2].start)
    own_tile = pltpu.make_async_copy(packed.at[u], tiles.at[u], tile_recv.at[0])
    own_tile.start()

    def beside_zero(side):
        beside[side] = jnp.zeros(beside.shape[1:], bf16)

    pl.when(jnp.logical_not(below))(lambda: beside_zero(0))
    pl.when(jnp.logical_not(above))(lambda: beside_zero(1))

    for slot in range(4):
        pl.when(meta_from[slot])(metas[slot].wait_recv)
    cell = jnp.concatenate([meta[i, 0:1, :] for i in range(5)], axis=1)
    observed = jnp.concatenate([meta[i, 1:2, :] for i in range(5)], axis=1)
    valid = (None,) + meta_from
    precision = jnp.concatenate(
        [meta[0, 2:3, :]] + [jnp.where(valid[i], meta[i, 2:3, :], 0.0) for i in range(1, 5)], axis=1
    )
    cell_row = jnp.floor(cell * (1.0 / W))
    cell_col = cell - W * cell_row

    def spread_out(shifts):
        return jnp.concatenate([jnp.full((1, n_obs), s, f32) for s in shifts], axis=1)

    ext_row = cell_row + spread_out((0.0, -float(rows), float(rows), 0.0, 0.0))
    ext_col = cell_col + spread_out((0.0, 0.0, 0.0, -float(W), float(W)))
    block = lax.bitwise_and(lax.broadcasted_iota(i32, (8, n_ext), 0), rows - 1).astype(f32)
    row_gap = (ext_row - block) * (1.0 / LOC_ROWS)
    col_gap = (ext_col - 0.5 * (W - 1)) * (1.0 / LOC_COLS)
    weight = member * jnp.exp(-0.5 * (row_gap * row_gap + col_gap * col_gap)) * precision
    select = (lax.broadcasted_iota(i32, (W, n_ext), 0).astype(f32) == cell_col).astype(f32).astype(bf16)
    lane, sub = lax.broadcasted_iota(i32, (8, W), 1), lax.broadcasted_iota(i32, (8, W), 0)
    lane_block = lax.bitwise_and(lane // ens, rows - 1)
    picks = [lane - lax.bitwise_and(lane, ens - 1) + k for k in range(ens)]
    unit = [(lax.bitwise_and(lane, ens - 1) == sub + 8 * h).astype(f32) for h in range(2)]
    in_block = [lane_block == r for r in range(rows)]
    of_row = [lax.bitwise_and(sub, rows - 1) == r for r in range(rows)]
    mine = lane_block == lax.bitwise_and(sub, rows - 1)
    in_row = [cell_row == float(r) for r in range(rows - 1)]
    pl.when(below)(pltpu.make_async_copy(beside.at[0], beside.at[0], tile_recv.at[1]).wait)
    pl.when(above)(pltpu.make_async_copy(beside.at[1], beside.at[1], tile_recv.at[2]).wait)
    pltpu.make_async_copy(packed, tiles, tile_recv.at[0]).wait()

    def flat(x):
        return x.reshape(big, x.shape[-1])

    for at in range(4):
        laid[at] = flat(tiles[:, :, at * W : (at + 1) * W]).astype(f32)
    for side in range(2):
        laid[4 + side] = flat(beside[side]).astype(f32)
    by_row = [[laid[at, pl.ds(r, ens, stride=rows), :] for at in range(6)] for r in range(rows)]
    obs = []
    for i, at in enumerate((1, 4, 5, 0, 2)):
        x = jnp.concatenate([q[at] for q in by_row], axis=0)
        here_obs = slice(i * n_obs, (i + 1) * n_obs)
        x = matmul(x.astype(bf16), select[:, here_obs])
        best = x[(rows - 1) * ens : rows * ens]
        for r in range(rows - 1):
            best = jnp.where(in_row[r][:, here_obs], x[r * ens : (r + 1) * ens], best)
        obs.append(best)
    obs = jnp.concatenate(obs, axis=1)
    obs_mean = jnp.sum(obs[0:8] + obs[8:16], axis=0, keepdims=True) * (1.0 / ens)
    spread = obs - obs_mean
    innovation = jnp.broadcast_to(observed - obs_mean, (8, n_ext))
    w_high, w_low = halves(jnp.concatenate([spread * weight[r : r + 1] for r in range(rows)], axis=0))
    s_high, s_low = halves(jnp.concatenate([spread] * 8 + [innovation], axis=0))
    across = ((1,), (1,))
    two = matmul(jnp.concatenate([w_high, w_low], axis=0), s_high, across)
    sums = two[0:big] + (two[big : 2 * big] + matmul(w_high, s_low, across))
    forcing = jnp.broadcast_to(sums[:, W : W + 1], (big, W))
    gram = []
    for h in range(2):
        part = sums[8 * h : 8 * h + 8, 0:W]
        for r in range(1, rows):
            part = jnp.where(in_block[r], sums[r * ens + 8 * h : r * ens + 8 * h + 8, 0:W], part)
        gram.append(part)

    anomalies, centre = [], jnp.zeros((8, 2 * W), f32)
    for r in range(rows):
        x = jnp.concatenate([by_row[r][1], by_row[r][3]], axis=1)
        mean = jnp.sum(x[0:8] + x[8:16], axis=0, keepdims=True) * (1.0 / ens)
        anomalies.append(x - mean)
        centre = jnp.where(jnp.concatenate([of_row[r]] * 2, axis=1), jnp.broadcast_to(mean, (8, 2 * W)), centre)
    e_high, e_low = halves(jnp.concatenate([jnp.concatenate(anomalies, axis=0), forcing], axis=1))
    extra = jnp.concatenate([e_high, e_low], axis=0)

    def combined(p, x, q, y):
        return [p * a + q * b for a, b in zip(x, y)]

    columns = columns_of(gram, picks)
    row_sums = [tree([jnp.abs(c) for c in half]) for half in columns]
    top = jnp.max(jnp.maximum(row_sums[0], row_sums[1]), axis=0, keepdims=True)
    bound = (ens - 1.0) + jnp.broadcast_to(top, (8, W))
    scale = 1.0 / bound
    end_scale = 1.0 / jnp.sqrt(bound)

    def system_times(x):
        return [scale * y for y in combined(ens - 1.0, x, 1.0, product(columns, x))]

    joint = [scale * y for y in combined(ens - 1.0, unit, 1.0, gram)]
    lower = combined(1.5, unit, -0.5, joint)
    half_way = combined(1.5, joint, -0.5, system_times(joint))
    joint = combined(1.5, half_way, -0.5, system_times(half_way))
    for step in range(1, NS_ITERS - 1):
        columns = columns_of(joint, picks)
        half_way = combined(1.5, joint, -0.5, product(columns, joint))
        lower = combined(1.5, lower, -0.5, product(columns, lower))
        joint = combined(1.5, half_way, -0.5, product(columns, half_way))
    root = combined(1.5, lower, -0.5, product(columns_of(lower, picks), joint))
    root = [x * end_scale for x in root]
    root_rows = []
    for v in range(big // 8):
        side, at = root[v // 4], (2 * v) % 8
        pair = jnp.where(
            sub < rows,
            jnp.broadcast_to(side[at : at + 1], (8, W)),
            jnp.broadcast_to(side[at + 1 : at + 2], (8, W)),
        )
        root_rows.append(jnp.where(mine, pair, 0.0))
    r_high, r_low = halves(jnp.concatenate(root_rows, axis=0))
    two = matmul(jnp.concatenate([r_high, r_low], axis=0), extra)
    rooted = two[0:big] + two[big : 2 * big]
    turned, half_shift = rooted[:, 0 : 2 * W], rooted[:, 2 * W : 3 * W]
    half_shift = jnp.concatenate([half_shift, half_shift], axis=1)
    shift = jnp.sum((turned * half_shift).reshape(n_mem, 8, 2 * W), axis=0)
    base = centre + shift + pltpu.roll(shift, rows, 0)
    updated = (math.sqrt(ens - 1.0) * turned).reshape(n_mem, 8, 2 * W) + base[None]
    for j in range(members):
        for var in range(2):
            moved[:, j, var] = updated[:, j * rows : (j + 1) * rows, var * W : (var + 1) * W].astype(bf16)

    def here(k):
        return out_ref.at[:, :, :, pl.ds(pl.multiple_of(k * W, W), W)]

    def back_copy(mem):
        return pltpu.make_async_remote_copy(
            src_ref=moved.at[mem], dst_ref=here(u),
            send_sem=back_send, recv_sem=back_recv,
            device_id={"mem": mem, "lat": t}, device_id_type=MESH,
        )

    own_back = pltpu.make_async_copy(moved.at[u], here(u), back_recv)

    def send_back(k, carry):
        back_copy(partner(k)).start()
        return carry

    lax.fori_loop(0, n_mem - 1, send_back, 0)
    own_back.start()

    others = pl.ds(0, n_mem - 1)
    pltpu.make_async_copy(packed.at[others], tiles.at[others], tile_send.at[0]).wait()
    pl.when(above)(pltpu.make_async_copy(beside.at[0], beside.at[0], tile_send.at[1]).wait)
    pl.when(below)(pltpu.make_async_copy(beside.at[1], beside.at[1], tile_send.at[2]).wait)
    for step, to, _ in halo_steps:
        pl.when(to)(lambda: each(halo_copies(step), "wait_send"))
    for slot in range(4):
        pl.when(meta_to[slot])(metas[slot].wait_send)
    pltpu.make_async_copy(moved.at[others], moved.at[others], back_send).wait()
    pltpu.make_async_copy(out_ref, out_ref, back_recv).wait()


def compact_call(n_mem, n_lat, prior, wind, cell, value, prec, nb, cnt):
    members, _, rows, cols = prior.shape
    n_obs = cell.shape[1]
    f32, bf16 = jnp.float32, jnp.bfloat16
    dma = pltpu.SemaphoreType.DMA
    return pl.pallas_call(
        functools.partial(kernel_compact, n_mem, n_lat),
        out_shape=pltpu.VMEM(prior.shape, bf16),
        in_specs=[pl.BlockSpec(memory_space=pl.ANY)] * 7,
        out_specs=pl.BlockSpec(memory_space=pltpu.VMEM),
        scratch_shapes=[
            pltpu.VMEM((3,) + prior.shape, bf16),
            pltpu.VMEM((3,) + wind.shape, f32),
            pltpu.VMEM(cell.shape, jnp.int32),
            pltpu.VMEM(value.shape, f32),
            pltpu.VMEM(prec.shape, f32),
            pltpu.VMEM(nb.shape, jnp.int32),
            pltpu.VMEM(cnt.shape, jnp.int32),
            pltpu.VMEM((5, 8, n_obs), f32),
            pltpu.VMEM((n_mem, members * rows, 4 * W), bf16),
            pltpu.VMEM((n_mem, members * rows, 4 * W), bf16),
            pltpu.VMEM((2, n_mem, members * rows, W), bf16),
            pltpu.VMEM((n_mem, members, 2, rows, W), bf16),
            pltpu.VMEM((6, n_mem * members * rows, W), f32),
            dma((7,)), dma((3, 2)), dma((3, 2)), dma((4,)), dma((4,)),
            dma((3,)), dma((3,)), dma, dma, pltpu.SemaphoreType.REGULAR((3,)),
        ],
        compiler_params=pltpu.CompilerParams(collective_id=0, has_side_effects=True),
    )(prior, wind, cell, value, prec, nb, cnt)


def on_device(n_mem, n_lat, *args):
    prior, wind, cell, value, prec, nb, cnt = args
    cnt = cnt.T
    members, _, rows, cols = prior.shape
    if members * n_mem == 16 and members == 2 and rows == 4:
        return compact_call(n_mem, n_lat, prior, wind, cell, value, prec, nb, cnt)
    n_obs = cell.shape[1]
    f32, bf16, i32 = jnp.float32, jnp.bfloat16, jnp.int32
    dma = pltpu.SemaphoreType.DMA
    return pl.pallas_call(
        functools.partial(kernel, n_mem, n_lat),
        out_shape=pltpu.VMEM(prior.shape, bf16),
        in_specs=[pl.BlockSpec(memory_space=pl.ANY)] * 7,
        out_specs=pl.BlockSpec(memory_space=pltpu.VMEM),
        scratch_shapes=[
            pltpu.VMEM((3,) + prior.shape, bf16),
            pltpu.VMEM((3,) + wind.shape, f32),
            pltpu.VMEM(cell.shape, i32),
            pltpu.VMEM(value.shape, f32),
            pltpu.VMEM(prec.shape, f32),
            pltpu.VMEM(nb.shape, i32),
            pltpu.VMEM(cnt.shape, i32),
            pltpu.VMEM((5, 8, n_obs), f32),
            pltpu.VMEM((n_mem, members * rows, 4 * W), bf16),
            pltpu.VMEM((n_mem, members * rows, 4 * W), bf16),
            pltpu.VMEM((2, n_mem, members * rows, W), bf16),
            pltpu.VMEM((n_mem, members, 2, rows, W), bf16),
            dma((7,)), dma((2, 2)), dma((2, 2)), dma((4,)), dma((4,)),
            dma((3, n_mem)), dma((3, n_mem)), dma((n_mem,)), dma((n_mem,)), pltpu.SemaphoreType.REGULAR,
        ],
        compiler_params=pltpu.CompilerParams(collective_id=0, has_side_effects=True),
    )(prior, wind, cell, value, prec, nb, cnt)


def solution(mesh):
    placed = (
        P("mem", None, "lat", None),
        P(None, "lat", None),
        P("lat", "mem"),
        P("lat", "mem"),
        P("lat", "mem"),
        P("lat", "mem", None),
        P("lat", "mem"),
    )
    return jax.shard_map(
        functools.partial(on_device, mesh.shape["mem"], mesh.shape["lat"]),
        mesh=mesh,
        in_specs=placed,
        out_specs=P("mem", None, "lat", None),
        check_vma=False,
    )
```

```python
import functools
import math

import jax
import jax.numpy as jnp
from jax import lax
from jax.experimental import pallas as pl
from jax.experimental.pallas import tpu as pltpu
from jax.sharding import PartitionSpec as P

W = 128
SECTIONS = 4
NS_ITERS = 6
LOC_ROWS = 2
LOC_COLS = 64
KAPPA = (0.025, 0.0125)
MESH = pl.DeviceIdType.MESH


def matmul(a, b, contract=((1,), (0,))):
    return lax.dot_general(a, b, (contract, ((), ())), preferred_element_type=jnp.float32)


def halves(x):
    high = x.astype(jnp.bfloat16)
    return high, (x - high.astype(jnp.float32)).astype(jnp.bfloat16)


def hp(a, b, contract=((1,), (0,))):
    a_high, a_low = halves(a)
    b_high, b_low = halves(b)
    return matmul(a_high, b_high, contract) + (
        matmul(a_high, b_low, contract) + matmul(a_low, b_high, contract)
    )


def kernel(
    n_mem, n_lat,
    prior_hbm, wind_hbm, cell_hbm, value_hbm, prec_hbm, nb_hbm, cnt_hbm,
    out_ref,
    prior, wind, cells, value, prec, nb, cnt, meta, packed, tiles, beside, moved,
    load_sem, halo_send, halo_recv, meta_send, meta_recv, tile_send, tile_recv, back_send, back_recv, ready,
):
    f32, bf16, i32 = jnp.float32, jnp.bfloat16, jnp.int32
    u = lax.axis_index("mem")
    t = lax.axis_index("lat")
    members, _, rows, cols = prior_hbm.shape
    slots = nb_hbm.shape[2]
    n_obs = cell_hbm.shape[1]
    ens = members * n_mem
    big = ens * rows
    half = members * rows

    lat_up, lat_down, mem_up, mem_down = t + 1, t - 1, u + 1, u - 1
    above, below = t < n_lat - 1, t > 0
    east_of, west_of = u < n_mem - 1, u > 0
    lats = 1 + above.astype(i32) + below.astype(i32)

    def partner(k):
        up = k + (k >= u).astype(i32)
        k = n_mem - 1 - k
        return jnp.where(2 * u >= n_mem, up, k - (k <= u).astype(i32))

    def signal(sem, mem, lat):
        pl.semaphore_signal(sem, inc=1, device_id={"mem": mem, "lat": lat}, device_id_type=MESH)

    def signal_lats(sem, mem):
        signal(sem, mem, t)
        pl.when(above)(lambda: signal(sem, mem, lat_up))
        pl.when(below)(lambda: signal(sem, mem, lat_down))

    loads = [
        pltpu.make_async_copy(src, dst, load_sem.at[i])
        for i, (src, dst) in enumerate((
            (prior_hbm, prior.at[1]), (wind_hbm, wind.at[1]), (cell_hbm, cells), (value_hbm, value),
            (prec_hbm, prec), (nb_hbm, nb), (cnt_hbm, cnt),
        ))
    ]
    for load in loads:
        load.start()

    barrier = pltpu.get_barrier_semaphore()
    pl.when(above)(lambda: signal(barrier, u, lat_up))
    pl.when(below)(lambda: signal(barrier, u, lat_down))

    def greet(d, carry):
        signal_lats(barrier, n_mem - 1 - d)
        return carry

    lax.fori_loop(0, n_mem - 1 - u, greet, 0)
    pl.semaphore_wait(barrier, lats * (u + 1) - 1)
    for load in loads[:2]:
        load.wait()

    def halo_copies(side, lat):
        return [
            pltpu.make_async_remote_copy(
                src_ref=src, dst_ref=dst.at[2 * side],
                send_sem=halo_send.at[side, kind], recv_sem=halo_recv.at[side, kind],
                device_id={"mem": u, "lat": lat}, device_id_type=MESH,
            )
            for kind, (src, dst) in enumerate(((prior.at[1], prior), (wind.at[1], wind)))
        ]

    def each(copies, act):
        for copy in copies:
            getattr(copy, act)()

    up_halo, down_halo = halo_copies(0, lat_up), halo_copies(1, lat_down)
    pl.when(above)(lambda: each(up_halo, "start"))
    pl.when(below)(lambda: each(down_halo, "start"))

    def answer(mem, carry):
        signal_lats(ready, mem)
        return carry

    lax.fori_loop(0, u, answer, 0)

    for load in loads[2:]:
        load.wait()
    meta[0, 0:1, :] = cells[...].astype(f32)
    meta[0, 1:2, :] = value[...]
    meta[0, 2:3, :] = prec[...]
    meta[0, 3:8, :] = jnp.zeros((5, n_obs), f32)
    metas = [
        pltpu.make_async_remote_copy(
            src_ref=meta.at[0], dst_ref=meta.at[slot + 1],
            send_sem=meta_send.at[slot], recv_sem=meta_recv.at[slot],
            device_id={"mem": mem, "lat": lat}, device_id_type=MESH,
        )
        for slot, (mem, lat) in enumerate(((u, lat_up), (u, lat_down), (mem_up, t), (mem_down, t)))
    ]
    meta_to = (above, below, east_of, west_of)
    meta_from = (below, above, west_of, east_of)

    def meta_zero(slot):
        meta[slot + 1] = jnp.zeros((8, n_obs), f32)

    for slot in (0, 1, 3):
        pl.when(meta_to[slot])(metas[slot].start)
    for slot in range(4):
        pl.when(jnp.logical_not(meta_from[slot]))(functools.partial(meta_zero, slot))

    n_ext = 5 * n_obs
    n_hi = n_ext // W
    listed = jnp.concatenate([nb[r] for r in range(rows)], axis=1)
    counts = jnp.concatenate(
        [jnp.broadcast_to(cnt[:, r : r + 1], (1, slots)) for r in range(rows)], axis=1
    )
    position = lax.broadcasted_iota(i32, (1, rows * slots), 1)
    hi = lax.shift_right_logical(listed, 7)
    lo = lax.bitwise_and(listed, W - 1)
    hi = jnp.where(lax.bitwise_and(position, slots - 1) < counts, hi, n_hi + 8)
    sub = lax.broadcasted_iota(i32, (8 * n_hi, rows * slots), 0)
    owner = position // slots
    key = hi * 8 + owner
    left = (sub == key).astype(f32) + (sub == key + rows).astype(f32)
    right = (lax.broadcasted_iota(i32, (W, rows * slots), 0) == lo).astype(f32)
    member = matmul(left.astype(bf16), right.astype(bf16), ((1,), (1,)))
    member = jnp.concatenate([member[8 * h : 8 * h + 8] for h in range(n_hi)], axis=1)

    pl.when(below)(lambda: each(up_halo, "wait_recv"))
    pl.when(above)(lambda: each(down_halo, "wait_recv"))
    wide = 4 * rows
    row_id = lax.broadcasted_iota(i32, (wide, cols), 0)
    col_id = lax.broadcasted_iota(i32, (wide, cols), 1)
    first_row = jnp.where(t == 0, rows, 0)
    last_row = jnp.where(t == n_lat - 1, 2 * rows, 3 * rows)
    inside = (row_id >= first_row) & (row_id < last_row)

    def band(parts):
        return jnp.concatenate(list(parts) + [jnp.zeros((rows, cols), f32)], axis=0)

    east = band(wind[s, 0] for s in range(3))
    north = band(wind[s, 1] for s in range(3))
    east_pos, east_neg = jnp.maximum(east, 0.0), jnp.minimum(east, 0.0)
    north_pos, north_neg = jnp.maximum(north, 0.0), jnp.minimum(north, 0.0)
    fields = []
    for var in range(2):
        kappa = KAPPA[var]
        keep = jnp.where(inside, 1.0 - (east_pos - east_neg + north_pos - north_neg) - 4.0 * kappa, 0.0)
        from_west = jnp.where(inside & (col_id > 0), east_pos + kappa, 0.0)
        from_east = jnp.where(inside & (col_id < cols - 1), kappa - east_neg, 0.0)
        from_south = jnp.where(inside, north_pos + kappa, 0.0)
        from_north = jnp.where(inside, kappa - north_neg, 0.0)
        own = []
        for j in range(members):
            q = jnp.where(inside, band(prior[s, j, var].astype(f32) for s in range(3)), 0.0)
            for _ in range(SECTIONS):
                q = (
                    keep * q
                    + from_west * pltpu.roll(q, 1, 1)
                    + from_east * pltpu.roll(q, cols - 1, 1)
                    + from_south * pltpu.roll(q, 1, 0)
                    + from_north * pltpu.roll(q, wide - 1, 0)
                )
            own.append(q[rows : 2 * rows])
        fields.append(jnp.concatenate(own, axis=0).astype(bf16))
    for k in range(n_mem):
        for place, (var, tile) in enumerate(((0, (k - 1) % n_mem), (0, k), (0, (k + 1) % n_mem), (1, k))):
            packed[k, :, place * W : (place + 1) * W] = fields[var][:, tile * W : (tile + 1) * W]

    def beside_copy(mem, side, lat):
        return pltpu.make_async_remote_copy(
            src_ref=packed.at[mem, :, pl.ds(W, W)], dst_ref=beside.at[side, u],
            send_sem=tile_send.at[1 + side, mem], recv_sem=tile_recv.at[1 + side, u],
            device_id={"mem": mem, "lat": lat}, device_id_type=MESH,
        )

    def tile_copy(mem):
        return pltpu.make_async_remote_copy(
            src_ref=packed.at[mem], dst_ref=tiles.at[u],
            send_sem=tile_send.at[0, mem], recv_sem=tile_recv.at[0, u],
            device_id={"mem": mem, "lat": t}, device_id_type=MESH,
        )

    def beside_both(mem, act):
        pl.when(above)(lambda: getattr(beside_copy(mem, 0, lat_up), act)())
        pl.when(below)(lambda: getattr(beside_copy(mem, 1, lat_down), act)())

    pl.when(east_of)(lambda: pl.semaphore_wait(ready, lats * (n_mem - 1 - u)))
    pl.when(east_of)(metas[2].start)

    def send_tiles(k, carry):
        mem = partner(k)
        tile_copy(mem).start()
        beside_both(mem, "start")
        return carry

    lax.fori_loop(0, n_mem - 1, send_tiles, 0)
    beside_both(u, "start")
    own_tile = pltpu.make_async_copy(packed.at[u], tiles.at[u], tile_recv.at[0, u])
    own_tile.start()

    def beside_zero(side):
        beside[side] = jnp.zeros(beside.shape[1:], bf16)

    pl.when(jnp.logical_not(below))(lambda: beside_zero(0))
    pl.when(jnp.logical_not(above))(lambda: beside_zero(1))

    for slot in range(4):
        pl.when(meta_from[slot])(metas[slot].wait_recv)
    cell = jnp.concatenate([meta[i, 0:1, :] for i in range(5)], axis=1)
    observed = jnp.concatenate([meta[i, 1:2, :] for i in range(5)], axis=1)
    valid = (None,) + meta_from
    precision = jnp.concatenate(
        [meta[0, 2:3, :]] + [jnp.where(valid[i], meta[i, 2:3, :], 0.0) for i in range(1, 5)], axis=1
    )
    cell_row = jnp.floor(cell * (1.0 / W))
    cell_col = cell - W * cell_row

    def spread_out(shifts):
        return jnp.concatenate([jnp.full((1, n_obs), s, f32) for s in shifts], axis=1)

    ext_row = cell_row + spread_out((0.0, -float(rows), float(rows), 0.0, 0.0))
    ext_col = cell_col + spread_out((0.0, 0.0, 0.0, -float(W), float(W)))
    block = lax.bitwise_and(lax.broadcasted_iota(i32, (8, n_ext), 0), rows - 1).astype(f32)
    row_gap = (ext_row - block) * (1.0 / LOC_ROWS)
    col_gap = (ext_col - 0.5 * (W - 1)) * (1.0 / LOC_COLS)
    weight = member * jnp.exp(-0.5 * (row_gap * row_gap + col_gap * col_gap)) * precision
    select = (lax.broadcasted_iota(i32, (W, n_ext), 0).astype(f32) == cell_col).astype(f32).astype(bf16)
    at_row = jnp.where(block == cell_row, 1.0, 0.0)
    ids0 = lax.broadcasted_iota(i32, (big, big), 0)
    ids1 = lax.broadcasted_iota(i32, (big, big), 1)
    same_member = (ids0 // rows == ids1 // rows).astype(f32).astype(bf16)
    same_block = lax.bitwise_and(ids0, rows - 1) == lax.bitwise_and(ids1, rows - 1)
    identity = (ids0 == ids1).astype(f32)

    own_tile.wait()

    def wait_tiles(k, carry):
        mem = partner(k)
        pltpu.make_async_copy(packed.at[0], tiles.at[mem], tile_recv.at[0, mem]).wait()
        return carry

    def wait_beside(side):
        def wait_one(mem, carry):
            pltpu.make_async_copy(
                packed.at[0, :, pl.ds(W, W)], beside.at[side, mem], tile_recv.at[1 + side, mem]
            ).wait()
            return carry

        lax.fori_loop(0, n_mem, wait_one, 0)

    lax.fori_loop(0, n_mem - 1, wait_tiles, 0)
    pl.when(below)(lambda: wait_beside(0))
    pl.when(above)(lambda: wait_beside(1))

    states = tiles[...].astype(f32)

    def flat(x):
        return x.reshape(big, x.shape[-1])

    sources = (
        states[:, :, W : 2 * W], beside[0].astype(f32), beside[1].astype(f32),
        states[:, :, 0:W], states[:, :, 2 * W : 3 * W],
    )
    picked = jnp.concatenate(
        [
            matmul(flat(x).astype(bf16), select[:, i * n_obs : (i + 1) * n_obs])
            for i, x in enumerate(sources)
        ],
        axis=1,
    )
    picked = picked.reshape(n_mem, 8, n_ext) * at_row[None]
    obs = matmul(same_member, flat(picked).astype(bf16))
    obs3 = obs.reshape(n_mem, 8, n_ext)
    folded = jnp.sum(obs3, axis=0)
    obs_mean = jnp.sum(folded, axis=0, keepdims=True) * (1.0 / big)
    spread = obs - obs_mean
    innovation = observed - obs_mean
    weighted = flat(spread.reshape(n_mem, 8, n_ext) * weight[None])
    gram = jnp.where(same_block, hp(weighted, spread, ((1,), (1,))), 0.0)
    forcing = jnp.sum(weighted * innovation, axis=1, keepdims=True)

    fields3 = jnp.concatenate([states[:, :, W : 2 * W], states[:, :, 3 * W : 4 * W]], axis=2)
    total = jnp.sum(fields3, axis=0)
    centre = (total + pltpu.roll(total, rows, 0)) * (1.0 / ens)
    anomalies = flat(fields3 - centre[None])
    extra = jnp.concatenate([anomalies, jnp.broadcast_to(forcing, (big, W))], axis=1)

    row_sums = jnp.broadcast_to(jnp.sum(jnp.abs(gram), axis=1, keepdims=True), (big, W))
    top = jnp.max(row_sums.reshape(n_mem, 8, W), axis=0)
    top = jnp.maximum(top, pltpu.roll(top, rows, 0))
    bound = (ens - 1.0) + jnp.broadcast_to(top[None], (n_mem, 8, W)).reshape(big, W)[:, 0:1]
    upper = ((ens - 1.0) * identity + gram) / bound
    factor = 1.5 * identity - 0.5 * upper
    lower = factor
    upper = hp(upper, factor)
    for step in range(1, NS_ITERS):
        factor = 1.5 * identity - 0.5 * hp(lower, upper)
        if step < NS_ITERS - 1:
            upper = hp(upper, factor)
            lower = hp(factor, lower)
    rooted = hp(factor, hp(lower, extra)) / jnp.sqrt(bound)
    turned, half_shift = rooted[:, 0 : 2 * W], rooted[:, 2 * W : 2 * W + 1]
    shift = jnp.sum((turned * half_shift).reshape(n_mem, 8, 2 * W), axis=0)
    base = centre + shift + pltpu.roll(shift, rows, 0)
    updated = (math.sqrt(ens - 1.0) * turned).reshape(n_mem, 8, 2 * W) + base[None]
    for j in range(members):
        for var in range(2):
            moved[:, j, var] = updated[:, j * rows : (j + 1) * rows, var * W : (var + 1) * W].astype(bf16)

    def here(k):
        return out_ref.at[:, :, :, pl.ds(pl.multiple_of(k * W, W), W)]

    def back_copy(mem):
        return pltpu.make_async_remote_copy(
            src_ref=moved.at[mem], dst_ref=here(u),
            send_sem=back_send.at[mem], recv_sem=back_recv.at[u],
            device_id={"mem": mem, "lat": t}, device_id_type=MESH,
        )

    own_back = pltpu.make_async_copy(moved.at[u], here(u), back_recv.at[u])

    def send_back(k, carry):
        back_copy(partner(k)).start()
        return carry

    lax.fori_loop(0, n_mem - 1, send_back, 0)
    own_back.start()

    def drain(k, carry):
        mem = partner(k)
        tile_copy(mem).wait_send()
        beside_both(mem, "wait_send")
        return carry

    lax.fori_loop(0, n_mem - 1, drain, 0)
    beside_both(u, "wait_send")
    pl.when(above)(lambda: each(up_halo, "wait_send"))
    pl.when(below)(lambda: each(down_halo, "wait_send"))
    for slot in range(4):
        pl.when(meta_to[slot])(metas[slot].wait_send)
    own_back.wait()

    def wait_back(k, carry):
        mem = partner(k)
        back_copy(mem).wait_send()
        pltpu.make_async_copy(moved.at[mem], here(mem), back_recv.at[mem]).wait()
        return carry

    lax.fori_loop(0, n_mem - 1, wait_back, 0)


def tree(terms):
    while len(terms) > 1:
        terms = [terms[i] + terms[i + 1] for i in range(0, len(terms), 2)]
    return terms[0]


def columns_of(pair, picks):
    return [[jnp.take_along_axis(x, pick, axis=1, mode="promise_in_bounds") for pick in picks] for x in pair]


def product(columns, pair):
    spread_rows = [jnp.broadcast_to(pair[k // 8][k % 8 : k % 8 + 1], (8, W)) for k in range(16)]
    return [tree([a * b for a, b in zip(half, spread_rows)]) for half in columns]


def kernel_compact(
    n_mem, n_lat,
    prior_hbm, wind_hbm, cell_hbm, value_hbm, prec_hbm, nb_hbm, cnt_hbm,
    out_ref,
    prior, wind, cells, value, prec, nb, cnt, meta, packed, tiles, beside, moved, laid,
    load_sem, halo_send, halo_recv, meta_send, meta_recv, tile_send, tile_recv, back_send, back_recv, ready,
):
    f32, bf16, i32 = jnp.float32, jnp.bfloat16, jnp.int32
    u = lax.axis_index("mem")
    t = lax.axis_index("lat")
    members, _, rows, cols = prior_hbm.shape
    slots = nb_hbm.shape[2]
    n_obs = cell_hbm.shape[1]
    ens = members * n_mem
    big = ens * rows
    half = members * rows

    lat_up, lat_down, mem_up, mem_down = t + 1, t - 1, u + 1, u - 1
    above, below = t < n_lat - 1, t > 0
    east_of, west_of = u < n_mem - 1, u > 0
    lats = 1 + above.astype(i32) + below.astype(i32)

    def partner(k):
        up = k + (k >= u).astype(i32)
        k = n_mem - 1 - k
        return jnp.where(2 * u >= n_mem, up, k - (k <= u).astype(i32))

    def signal(sem, mem, lat):
        pl.semaphore_signal(sem, inc=1, device_id={"mem": mem, "lat": lat}, device_id_type=MESH)

    loads = [
        pltpu.make_async_copy(src, dst, load_sem.at[i])
        for i, (src, dst) in enumerate((
            (prior_hbm, prior.at[1]), (wind_hbm, wind.at[1]), (cell_hbm, cells), (value_hbm, value),
            (prec_hbm, prec), (nb_hbm, nb), (cnt_hbm, cnt),
        ))
    ]
    barrier = pltpu.get_barrier_semaphore()
    pl.when(above)(lambda: signal(barrier, u, lat_up))
    pl.when(below)(lambda: signal(barrier, u, lat_down))
    for load in loads[:2]:
        load.start()

    def greet(d, carry):
        mem = n_mem - 1 - d
        signal(barrier, mem, t)
        pl.when(above)(lambda: signal(barrier, mem, lat_up))
        pl.when(below)(lambda: signal(barrier, mem, lat_down))
        return carry

    lax.fori_loop(0, n_mem - 1 - u, greet, 0)
    pl.semaphore_wait(barrier, lats * (u + 1) - 1)
    def answer(mem, carry):
        pl.when(below)(lambda: signal(ready.at[2], mem, lat_down))
        signal(ready.at[0], mem, t)
        pl.when(above)(lambda: signal(ready.at[1], mem, lat_up))
        return carry

    lax.fori_loop(0, u, answer, 0)
    for load in loads[2:]:
        load.start()
    for load in loads[:2]:
        load.wait()

    def halo_copies(step):
        return [
            pltpu.make_async_remote_copy(
                src_ref=ref.at[1], dst_ref=ref.at[1 - step],
                send_sem=halo_send.at[1 - step, kind], recv_sem=halo_recv.at[1 - step, kind],
                device_id={"mem": u, "lat": t + step}, device_id_type=MESH,
            )
            for kind, ref in enumerate((prior, wind))
        ]

    def each(copies, act):
        for copy in copies:
            getattr(copy, act)()

    odd = lax.rem(t, 2) == 1
    halo_steps = ((1, above, below), (-1, below, above))
    pl.when(odd & above)(lambda: each(halo_copies(1), "start"))
    pl.when(below)(lambda: each(halo_copies(-1), "start"))
    pl.when(jnp.logical_not(odd) & above)(lambda: each(halo_copies(1), "start"))

    for load in loads[2:]:
        load.wait()
    meta[0, 0:1, :] = cells[...].astype(f32)
    meta[0, 1:2, :] = value[...]
    meta[0, 2:3, :] = prec[...]
    meta[0, 3:8, :] = jnp.zeros((5, n_obs), f32)
    metas = [
        pltpu.make_async_remote_copy(
            src_ref=meta.at[0], dst_ref=meta.at[slot + 1],
            send_sem=meta_send.at[slot], recv_sem=meta_recv.at[slot],
            device_id={"mem": mem, "lat": lat}, device_id_type=MESH,
        )
        for slot, (mem, lat) in enumerate(((u, lat_up), (u, lat_down), (mem_up, t), (mem_down, t)))
    ]
    meta_to = (above, below, east_of, west_of)
    meta_from = (below, above, west_of, east_of)

    def meta_zero(slot):
        meta[slot + 1] = jnp.zeros((8, n_obs), f32)

    for slot in (0, 1, 3):
        pl.when(meta_to[slot])(metas[slot].start)
    for slot in range(4):
        pl.when(jnp.logical_not(meta_from[slot]))(functools.partial(meta_zero, slot))

    for step, _, came in halo_steps:
        pl.when(came)(lambda: each(halo_copies(step), "wait_recv"))
    col_id = lax.broadcasted_iota(i32, (8, cols), 1)
    row_in = lax.bitwise_and(lax.broadcasted_iota(i32, (8, cols), 0), rows - 1)
    at_bottom, at_top = row_in == 0, row_in == rows - 1
    not_west, not_east = col_id > 0, col_id < cols - 1
    band_ok = [below, None, above]

    def masked(b, x):
        return x if band_ok[b] is None else jnp.where(band_ok[b], x, 0.0)

    flows = []
    for b in range(3):
        east, north = (jnp.concatenate([wind[b, way], wind[b, way]], axis=0) for way in range(2))
        flows.append((
            jnp.maximum(east, 0.0), jnp.minimum(east, 0.0), jnp.maximum(north, 0.0), jnp.minimum(north, 0.0),
        ))
    def forecast(var):
        kappa = KAPPA[var]
        bands = range(3)
        first_band, last_band = bands[0], bands[-1]
        coef, q = {}, {}
        for b in bands:
            east_pos, east_neg, north_pos, north_neg = flows[b]
            coef[b] = (
                masked(b, 1.0 - (east_pos - east_neg + north_pos - north_neg) - 4.0 * kappa),
                masked(b, jnp.where(not_west, east_pos + kappa, 0.0)),
                masked(b, jnp.where(not_east, kappa - east_neg, 0.0)),
                masked(b, north_pos + kappa),
                masked(b, kappa - north_neg),
            )
            q[b] = masked(b, jnp.concatenate([prior[b, j, var].astype(f32) for j in range(members)], axis=0))
        for s in range(1, SECTIONS + 1):
            new = {}
            for b in bands if s < SECTIONS else bands[1:-1]:
                keep, from_west, from_east, from_south, from_north = coef[b]
                south, north = pltpu.roll(q[b], 1, 0), pltpu.roll(q[b], 7, 0)
                if b > first_band:
                    south = jnp.where(at_bottom, pltpu.roll(q[b - 1], 5, 0), south)
                if b < last_band:
                    north = jnp.where(at_top, pltpu.roll(q[b + 1], 3, 0), north)
                new[b] = (
                    keep * q[b]
                    + from_west * pltpu.roll(q[b], 1, 1)
                    + from_east * pltpu.roll(q[b], cols - 1, 1)
                    + from_south * south
                    + from_north * north
                )
            q = new
        return q[1].astype(bf16)
    def pack(x, places):
        for k in range(n_mem):
            for place, tile in places(k):
                packed[k, :, place * W : (place + 1) * W] = x[:, tile * W : (tile + 1) * W]

    pack(forecast(0), lambda k: ((0, (k - 1) % n_mem), (1, k), (2, (k + 1) % n_mem)))

    share = (pl.ds(0, 3 * W), pl.ds(3 * W, W))
    share_sem = (0, 3)

    def tile_copy(mem, var):
        return pltpu.make_async_remote_copy(
            src_ref=packed.at[mem, :, share[var]], dst_ref=tiles.at[u, :, share[var]],
            send_sem=tile_send.at[share_sem[var]], recv_sem=tile_recv.at[share_sem[var]],
            device_id={"mem": mem, "lat": t}, device_id_type=MESH,
        )

    def beside_copy(mem, side):
        return pltpu.make_async_remote_copy(
            src_ref=packed.at[mem, :, pl.ds(W, W)], dst_ref=beside.at[side, u],
            send_sem=tile_send.at[1 + side], recv_sem=tile_recv.at[1 + side],
            device_id={"mem": mem, "lat": t + 1 - 2 * side}, device_id_type=MESH,
        )

    def known(at):
        pl.when(east_of)(lambda: pl.semaphore_wait(ready.at[at], n_mem - 1 - u))

    def send_beside(side):
        known(2 - side)

        for k in range(n_mem - 1):
            beside_copy(partner(k), side).start()
        beside_copy(u, side).start()

    pl.when(below)(lambda: send_beside(1))
    known(0)
    for k in range(n_mem - 1):
        tile_copy(partner(k), 0).start()
    pl.when(above)(lambda: send_beside(0))
    pl.when(east_of)(metas[2].start)
    pack(forecast(1), lambda k: ((3, k),))
    for k in range(n_mem - 1):
        tile_copy(partner(k), 1).start()
    for var in range(2):
        pltpu.make_async_copy(
            packed.at[u, :, share[var]], tiles.at[u, :, share[var]], tile_recv.at[share_sem[var]]
        ).start()

    def beside_zero(side):
        beside[side] = jnp.zeros(beside.shape[1:], bf16)

    pl.when(jnp.logical_not(below))(lambda: beside_zero(0))
    pl.when(jnp.logical_not(above))(lambda: beside_zero(1))

    n_ext = 5 * n_obs
    n_hi = n_ext // W
    listed = jnp.concatenate([nb[r] for r in range(rows)], axis=1)
    counts = jnp.concatenate(
        [jnp.broadcast_to(cnt[:, r : r + 1], (1, slots)) for r in range(rows)], axis=1
    )
    position = lax.broadcasted_iota(i32, (1, rows * slots), 1)
    hi = lax.shift_right_logical(listed, 7)
    lo = lax.bitwise_and(listed, W - 1)
    hi = jnp.where(lax.bitwise_and(position, slots - 1) < counts, hi, n_hi + 8)
    sub = lax.broadcasted_iota(i32, (8 * n_hi, rows * slots), 0)
    owner = position // slots
    key = hi * 8 + owner
    left = (sub == key).astype(f32) + (sub == key + rows).astype(f32)
    right = (lax.broadcasted_iota(i32, (W, rows * slots), 0) == lo).astype(f32)
    member = matmul(left.astype(bf16), right.astype(bf16), ((1,), (1,)))
    member = jnp.concatenate([member[8 * h : 8 * h + 8] for h in range(n_hi)], axis=1)

    for slot in range(4):
        pl.when(meta_from[slot])(metas[slot].wait_recv)
    cell = jnp.concatenate([meta[i, 0:1, :] for i in range(5)], axis=1)
    observed = jnp.concatenate([meta[i, 1:2, :] for i in range(5)], axis=1)
    valid = (None,) + meta_from
    precision = jnp.concatenate(
        [meta[0, 2:3, :]] + [jnp.where(valid[i], meta[i, 2:3, :], 0.0) for i in range(1, 5)], axis=1
    )
    cell_row = jnp.floor(cell * (1.0 / W))
    cell_col = cell - W * cell_row

    def spread_out(shifts):
        return jnp.concatenate([jnp.full((1, n_obs), s, f32) for s in shifts], axis=1)

    ext_row = cell_row + spread_out((0.0, -float(rows), float(rows), 0.0, 0.0))
    ext_col = cell_col + spread_out((0.0, 0.0, 0.0, -float(W), float(W)))
    block = lax.bitwise_and(lax.broadcasted_iota(i32, (8, n_ext), 0), rows - 1).astype(f32)
    row_gap = (ext_row - block) * (1.0 / LOC_ROWS)
    col_gap = (ext_col - 0.5 * (W - 1)) * (1.0 / LOC_COLS)
    weight = member * jnp.exp(-0.5 * (row_gap * row_gap + col_gap * col_gap)) * precision
    select = (lax.broadcasted_iota(i32, (W, n_ext), 0).astype(f32) == cell_col).astype(f32).astype(bf16)
    lane, sub = lax.broadcasted_iota(i32, (8, W), 1), lax.broadcasted_iota(i32, (8, W), 0)
    lane_block = lax.bitwise_and(lane // ens, rows - 1)
    picks = [lane - lax.bitwise_and(lane, ens - 1) + k for k in range(ens)]
    unit = [(lax.bitwise_and(lane, ens - 1) == sub + 8 * h).astype(f32) for h in range(2)]
    in_block = [lane_block == r for r in range(rows)]
    of_row = [lax.bitwise_and(sub, rows - 1) == r for r in range(rows)]
    mine = lane_block == lax.bitwise_and(sub, rows - 1)
    in_row = [cell_row == float(r) for r in range(rows - 1)]
    pl.when(below)(pltpu.make_async_copy(beside.at[0], beside.at[0], tile_recv.at[1]).wait)
    pl.when(above)(pltpu.make_async_copy(beside.at[1], beside.at[1], tile_recv.at[2]).wait)

    def wait_tiles(var):
        pltpu.make_async_copy(
            packed.at[:, :, share[var]], tiles.at[:, :, share[var]], tile_recv.at[share_sem[var]]
        ).wait()

    wait_tiles(0)

    def flat(x):
        return x.reshape(big, x.shape[-1])

    for at in range(3):
        laid[at] = flat(tiles[:, :, at * W : (at + 1) * W]).astype(f32)
    for side in range(2):
        laid[4 + side] = flat(beside[side]).astype(f32)
    by_row = [[laid[at, pl.ds(r, ens, stride=rows), :] for at in (0, 1, 2, 4, 5)] for r in range(rows)]
    obs = []
    for i, at in enumerate((1, 3, 4, 0, 2)):
        x = jnp.concatenate([q[at] for q in by_row], axis=0)
        here_obs = slice(i * n_obs, (i + 1) * n_obs)
        x = matmul(x.astype(bf16), select[:, here_obs])
        best = x[(rows - 1) * ens : rows * ens]
        for r in range(rows - 1):
            best = jnp.where(in_row[r][:, here_obs], x[r * ens : (r + 1) * ens], best)
        obs.append(best)
    obs = jnp.concatenate(obs, axis=1)
    obs_mean = jnp.sum(obs[0:8] + obs[8:16], axis=0, keepdims=True) * (1.0 / ens)
    spread = obs - obs_mean
    innovation = jnp.broadcast_to(observed - obs_mean, (8, n_ext))
    w_high, w_low = halves(jnp.concatenate([spread * weight[r : r + 1] for r in range(rows)], axis=0))
    s_high, s_low = halves(jnp.concatenate([spread] * 8 + [innovation], axis=0))
    across = ((1,), (1,))
    two = matmul(jnp.concatenate([w_high, w_low], axis=0), s_high, across)
    sums = two[0:big] + (two[big : 2 * big] + matmul(w_high, s_low, across))
    forcing = jnp.broadcast_to(sums[:, W : W + 1], (big, W))
    gram = []
    for h in range(2):
        part = sums[8 * h : 8 * h + 8, 0:W]
        for r in range(1, rows):
            part = jnp.where(in_block[r], sums[r * ens + 8 * h : r * ens + 8 * h + 8, 0:W], part)
        gram.append(part)

    def combined(p, x, q, y):
        return [p * a + q * b for a, b in zip(x, y)]

    columns = columns_of(gram, picks)
    row_sums = [tree([jnp.abs(c) for c in half]) for half in columns]
    top = jnp.max(jnp.maximum(row_sums[0], row_sums[1]), axis=0, keepdims=True)
    bound = (ens - 1.0) + jnp.broadcast_to(top, (8, W))
    scale = 1.0 / bound
    end_scale = 1.0 / jnp.sqrt(bound)

    def system_times(x):
        return [scale * y for y in combined(ens - 1.0, x, 1.0, product(columns, x))]

    joint = [scale * y for y in combined(ens - 1.0, unit, 1.0, gram)]
    lower = combined(1.5, unit, -0.5, joint)
    half_way = combined(1.5, joint, -0.5, system_times(joint))
    joint = combined(1.5, half_way, -0.5, system_times(half_way))
    for step in range(1, NS_ITERS - 1):
        columns = columns_of(joint, picks)
        half_way = combined(1.5, joint, -0.5, product(columns, joint))
        lower = combined(1.5, lower, -0.5, product(columns, lower))
        joint = combined(1.5, half_way, -0.5, product(columns, half_way))
    root = combined(1.5, lower, -0.5, product(columns_of(lower, picks), joint))
    root = [x * end_scale for x in root]
    wait_tiles(1)
    laid[3] = flat(tiles[:, :, 3 * W : 4 * W]).astype(f32)
    anomalies, centre = [], jnp.zeros((8, 2 * W), f32)
    for r in range(rows):
        x = jnp.concatenate([by_row[r][1], laid[3, pl.ds(r, ens, stride=rows), :]], axis=1)
        mean = jnp.sum(x[0:8] + x[8:16], axis=0, keepdims=True) * (1.0 / ens)
        anomalies.append(x - mean)
        centre = jnp.where(jnp.concatenate([of_row[r]] * 2, axis=1), jnp.broadcast_to(mean, (8, 2 * W)), centre)
    e_high, e_low = halves(jnp.concatenate([jnp.concatenate(anomalies, axis=0), forcing], axis=1))
    extra = jnp.concatenate([e_high, e_low], axis=0)

    root_rows = []
    for v in range(big // 8):
        side, at = root[v // 4], (2 * v) % 8
        pair = jnp.where(
            sub < rows,
            jnp.broadcast_to(side[at : at + 1], (8, W)),
            jnp.broadcast_to(side[at + 1 : at + 2], (8, W)),
        )
        root_rows.append(jnp.where(mine, pair, 0.0))
    r_high, r_low = halves(jnp.concatenate(root_rows, axis=0))
    two = matmul(jnp.concatenate([r_high, r_low], axis=0), extra)
    rooted = two[0:big] + two[big : 2 * big]
    turned, half_shift = rooted[:, 0 : 2 * W], rooted[:, 2 * W : 3 * W]
    half_shift = jnp.concatenate([half_shift, half_shift], axis=1)
    shift = jnp.sum((turned * half_shift).reshape(n_mem, 8, 2 * W), axis=0)
    base = centre + shift + pltpu.roll(shift, rows, 0)
    updated = (math.sqrt(ens - 1.0) * turned).reshape(n_mem, 8, 2 * W) + base[None]
    for j in range(members):
        for var in range(2):
            moved[:, j, var] = updated[:, j * rows : (j + 1) * rows, var * W : (var + 1) * W].astype(bf16)

    def here(k):
        return out_ref.at[:, :, :, pl.ds(pl.multiple_of(k * W, W), W)]

    def back_copy(mem):
        return pltpu.make_async_remote_copy(
            src_ref=moved.at[mem], dst_ref=here(u),
            send_sem=back_send, recv_sem=back_recv,
            device_id={"mem": mem, "lat": t}, device_id_type=MESH,
        )

    own_back = pltpu.make_async_copy(moved.at[u], here(u), back_recv)

    for k in range(n_mem - 1):
        back_copy(partner(k)).start()
    own_back.start()

    others = pl.ds(0, n_mem - 1)
    for var in range(2):
        pltpu.make_async_copy(
            packed.at[others, :, share[var]], tiles.at[others, :, share[var]], tile_send.at[share_sem[var]]
        ).wait()
    pl.when(above)(pltpu.make_async_copy(beside.at[0], beside.at[0], tile_send.at[1]).wait)
    pl.when(below)(pltpu.make_async_copy(beside.at[1], beside.at[1], tile_send.at[2]).wait)
    for step, to, _ in halo_steps:
        pl.when(to)(lambda: each(halo_copies(step), "wait_send"))
    for slot in range(4):
        pl.when(meta_to[slot])(metas[slot].wait_send)
    pltpu.make_async_copy(moved.at[others], moved.at[others], back_send).wait()
    pltpu.make_async_copy(out_ref, out_ref, back_recv).wait()


def compact_call(n_mem, n_lat, prior, wind, cell, value, prec, nb, cnt):
    members, _, rows, cols = prior.shape
    n_obs = cell.shape[1]
    f32, bf16 = jnp.float32, jnp.bfloat16
    dma = pltpu.SemaphoreType.DMA
    return pl.pallas_call(
        functools.partial(kernel_compact, n_mem, n_lat),
        out_shape=pltpu.VMEM(prior.shape, bf16),
        in_specs=[pl.BlockSpec(memory_space=pl.ANY)] * 7,
        out_specs=pl.BlockSpec(memory_space=pltpu.VMEM),
        scratch_shapes=[
            pltpu.VMEM((3,) + prior.shape, bf16),
            pltpu.VMEM((3,) + wind.shape, f32),
            pltpu.VMEM(cell.shape, jnp.int32),
            pltpu.VMEM(value.shape, f32),
            pltpu.VMEM(prec.shape, f32),
            pltpu.VMEM(nb.shape, jnp.int32),
            pltpu.VMEM(cnt.shape, jnp.int32),
            pltpu.VMEM((5, 8, n_obs), f32),
            pltpu.VMEM((n_mem, members * rows, 4 * W), bf16),
            pltpu.VMEM((n_mem, members * rows, 4 * W), bf16),
            pltpu.VMEM((2, n_mem, members * rows, W), bf16),
            pltpu.VMEM((n_mem, members, 2, rows, W), bf16),
            pltpu.VMEM((6, n_mem * members * rows, W), f32),
            dma((7,)), dma((3, 2)), dma((3, 2)), dma((4,)), dma((4,)),
            dma((4,)), dma((4,)), dma, dma, pltpu.SemaphoreType.REGULAR((3,)),
        ],
        compiler_params=pltpu.CompilerParams(collective_id=0, has_side_effects=True),
    )(prior, wind, cell, value, prec, nb, cnt)


def on_device(n_mem, n_lat, *args):
    prior, wind, cell, value, prec, nb, cnt = args
    cnt = cnt.T
    members, _, rows, cols = prior.shape
    if members * n_mem == 16 and members == 2 and rows == 4:
        return compact_call(n_mem, n_lat, prior, wind, cell, value, prec, nb, cnt)
    n_obs = cell.shape[1]
    f32, bf16, i32 = jnp.float32, jnp.bfloat16, jnp.int32
    dma = pltpu.SemaphoreType.DMA
    return pl.pallas_call(
        functools.partial(kernel, n_mem, n_lat),
        out_shape=pltpu.VMEM(prior.shape, bf16),
        in_specs=[pl.BlockSpec(memory_space=pl.ANY)] * 7,
        out_specs=pl.BlockSpec(memory_space=pltpu.VMEM),
        scratch_shapes=[
            pltpu.VMEM((3,) + prior.shape, bf16),
            pltpu.VMEM((3,) + wind.shape, f32),
            pltpu.VMEM(cell.shape, i32),
            pltpu.VMEM(value.shape, f32),
            pltpu.VMEM(prec.shape, f32),
            pltpu.VMEM(nb.shape, i32),
            pltpu.VMEM(cnt.shape, i32),
            pltpu.VMEM((5, 8, n_obs), f32),
            pltpu.VMEM((n_mem, members * rows, 4 * W), bf16),
            pltpu.VMEM((n_mem, members * rows, 4 * W), bf16),
            pltpu.VMEM((2, n_mem, members * rows, W), bf16),
            pltpu.VMEM((n_mem, members, 2, rows, W), bf16),
            dma((7,)), dma((2, 2)), dma((2, 2)), dma((4,)), dma((4,)),
            dma((3, n_mem)), dma((3, n_mem)), dma((n_mem,)), dma((n_mem,)), pltpu.SemaphoreType.REGULAR,
        ],
        compiler_params=pltpu.CompilerParams(collective_id=0, has_side_effects=True),
    )(prior, wind, cell, value, prec, nb, cnt)


def solution(mesh):
    placed = (
        P("mem", None, "lat", None),
        P(None, "lat", None),
        P("lat", "mem"),
        P("lat", "mem"),
        P("lat", "mem"),
        P("lat", "mem", None),
        P("lat", "mem"),
    )
    return jax.shard_map(
        functools.partial(on_device, mesh.shape["mem"], mesh.shape["lat"]),
        mesh=mesh,
        in_specs=placed,
        out_specs=P("mem", None, "lat", None),
        check_vma=False,
    )
```
